32 devices in a mesh: dp: 8 (over z, y), proto: 4 (over x, core).
Axes of the slice: x: 2, y: 2, z: 4, core: 2. Of those that a mesh axis runs over, the one named last changes fastest.
Arguments:
- teacher_feat: bfloat16 [1024, 128], P('dp'), may hold values from -32 to 32
- student_feat: bfloat16 [1024, 128], P('dp'), may hold values from -32 to 32
- proto_weight: bfloat16 [128, 32768], P(None, 'proto'), may hold values from -0.5 to 0.5
Outputs:
- proto_grad: float32 [128, 32768], P('dp', 'proto')
- feature_grad: float32 [1024, 128], P('dp')
The draws below stay inside these ranges and needn't reach their ends.
All inputs are finite; a program needn't handle non-finite values.
Results may differ from the reference program's by a relative error of at most 0.0028.
Values sent between devices are 32-bit elements; how exact they have to be, the bound alone decides.
No kernel may reach another device: no remote copies, remote signals or barrier semaphores. Data moves between devices by JAX's collectives and lax.ppermute only.
A program may use at most 64 MiB of HBM per device.

```python
import math
import jax
import jax.numpy as jnp
from jax import lax

D = 128
K = 32768
ROWS_DEV = 128
ITERS = 3
ROWS = 1024
N_DP = 8


def base_weight(key):
    first_key = jax.random.fold_in(key, 7)
    values = jax.random.normal(first_key, (D, K), jnp.float32)
    return values / math.sqrt(D)


def draw_proto_weight(key, part):
    return base_weight(key).astype(jnp.bfloat16)


def view_feature_vectors(key, stochastic_shift):
    subkeys = jax.random.split(jax.random.fold_in(key, stochastic_shift), 1)
    values = jax.random.normal(subkeys[0], (ROWS, D), jnp.float32)
    return values.astype(jnp.bfloat16)


def draw_teacher_feat(key, part):
    return view_feature_vectors(key, 21)


def draw_student_feat(key, part):
    return view_feature_vectors(key, 33)


def setup_inputs(seed: int = 0) -> dict:
    key_list = jax.random.split(jax.random.key(seed), 4)
    return {
        "teacher_feat": draw_teacher_feat(jax.random.fold_in(key_list[3], 71), 0),
        "student_feat": draw_student_feat(jax.random.fold_in(key_list[3], 71), 0),
        "proto_weight": draw_proto_weight(jax.random.fold_in(key_list[3], 71), 0),
    }


teacher_temp = 0.07
student_temp = 0.1


def divided_logits(feature_vector_count, broadened_center_matrix, logit_sharpness_divisor):
    product_matrix = jnp.dot(feature_vector_count.astype(jnp.float32), broadened_center_matrix, precision=lax.Precision.HIGHEST, preferred_element_type=jnp.float32)
    return product_matrix / logit_sharpness_divisor


def reference(teacher_feat, student_feat, proto_weight):
    broadened_center_matrix = proto_weight.astype(jnp.float32)
    teacher_blocks = teacher_feat.reshape(N_DP, ROWS_DEV, D)
    student_blocks = student_feat.reshape(N_DP, ROWS_DEV, D)

    def block_peak(tblock):
        return jnp.max(divided_logits(tblock, broadened_center_matrix, teacher_temp), axis=1)

    teacher_peak = lax.map(block_peak, teacher_blocks)

    def kernel(tblock, peak):
        return jnp.exp(divided_logits(tblock, broadened_center_matrix, teacher_temp) - peak[:, None])

    row_scale = jnp.ones((N_DP, ROWS_DEV), jnp.float32)
    col_scale = jnp.ones((K,), jnp.float32)
    for sweep in range(ITERS):
        def add_columns(carry, items):
            tblock, peak, scale = items
            return carry + jnp.sum(kernel(tblock, peak) * scale[:, None], axis=0), None

        col_total, unused = lax.scan(add_columns, jnp.zeros((K,), jnp.float32), (teacher_blocks, teacher_peak, row_scale))
        col_scale = 1.0 / col_total

        def row_total(items):
            tblock, peak = items
            return jnp.sum(kernel(tblock, peak) * col_scale[None, :], axis=1)

        row_scale = 1.0 / lax.map(row_total, (teacher_blocks, teacher_peak))

    def block_grads(carry, items):
        tblock, sblock, peak, scale = items
        target = kernel(tblock, peak) * scale[:, None] * col_scale[None, :]
        student_scores = divided_logits(sblock, broadened_center_matrix, student_temp)
        student_peak = jnp.max(student_scores, axis=1, keepdims=True)
        raised = jnp.exp(student_scores - student_peak)
        student_probs = raised / jnp.sum(raised, axis=1, keepdims=True)
        grad_scores = ((student_probs - target) / student_temp).astype(jnp.bfloat16)
        grad_wide = grad_scores.astype(jnp.float32)
        input_grad = lax.dot_general(grad_wide, broadened_center_matrix, (((1,), (1,)), ((), ())), precision=lax.Precision.HIGHEST, preferred_element_type=jnp.float32)
        update = lax.dot_general(sblock.astype(jnp.float32), grad_wide, (((0,), (0,)), ((), ())), precision=lax.Precision.HIGHEST, preferred_element_type=jnp.float32)
        return carry + update, input_grad

    proto_grad, input_grads = lax.scan(block_grads, jnp.zeros((D, K), jnp.float32), (teacher_blocks, student_blocks, teacher_peak, row_scale))
    return proto_grad, input_grads.reshape(ROWS, D)
```

```python
import math

import jax
import jax.numpy as jnp
from jax import lax
from jax.experimental import pallas as pl
from jax.experimental.pallas import tpu as pltpu
from jax.sharding import PartitionSpec as P

ITERS = 3

teacher_temp = 0.07
student_temp = 0.1

LOG2E = math.log2(math.e)
T_EXP = LOG2E / teacher_temp
S_EXP = LOG2E / student_temp

LANES = 128
SUB = 8
PARTS = 4
STAT_ROWS = 8
KERNEL_BYTES = 32 << 20


def combined_all(value, axis, combine):
    everything = jax.tree.map(lambda part: lax.all_gather(part, axis), value)
    leading = jax.tree.map(lambda part: part[0], everything)

    def step(k, so_far):
        return combine(so_far, jax.tree.map(lambda part: part[k], everything))

    return lax.fori_loop(1, lax.axis_size(axis), step, leading)


def divided_logits(features, prototypes, divisor):
    return jnp.dot(features, prototypes, preferred_element_type=jnp.float32) / divisor


def combine_stats(earlier, later):
    teacher_peak = jnp.maximum(earlier[0], later[0])
    student_peak = jnp.maximum(earlier[1], later[1])
    merged_total = earlier[2] * jnp.exp(earlier[1] - student_peak) + later[2] * jnp.exp(
        later[1] - student_peak
    )
    return (teacher_peak, student_peak, merged_total)


def split_crops(teacher_feat, student_feat, proto_weight):
    teacher_scores = divided_logits(teacher_feat, proto_weight, teacher_temp)
    student_scores = divided_logits(student_feat, proto_weight, student_temp)
    local_teacher = jnp.max(teacher_scores, axis=1)
    local_student = jnp.max(student_scores, axis=1)
    local_total = jnp.sum(jnp.exp(student_scores - local_student[:, None]), axis=1)
    teacher_peak, student_peak, student_total = combined_all(
        (local_teacher, local_student, local_total), "proto", combine_stats
    )
    kernel = jnp.exp(teacher_scores - teacher_peak[:, None])
    row_scale = jnp.ones((teacher_feat.shape[0],), jnp.float32)
    for sweep in range(ITERS):
        col_part = jnp.sum(kernel * row_scale[:, None], axis=0)
        col_scale = 1.0 / lax.psum(col_part, "dp")
        row_part = jnp.sum(kernel * col_scale[None, :], axis=1)
        row_scale = 1.0 / lax.psum(row_part, "proto")
    target = kernel * row_scale[:, None] * col_scale[None, :]
    student_probs = jnp.exp(student_scores - student_peak[:, None]) / student_total[:, None]
    grad_scores = ((student_probs - target) / student_temp).astype(jnp.bfloat16)
    input_part = lax.dot_general(
        grad_scores, proto_weight, (((1,), (1,)), ((), ())), preferred_element_type=jnp.float32
    )
    feature_grad = lax.psum(input_part, "proto")
    proto_grad = lax.psum_scatter(
        lax.dot_general(
            student_feat, grad_scores, (((0,), (0,)), ((), ())), preferred_element_type=jnp.float32
        ),
        "dp",
        scatter_dimension=0,
        tiled=True,
    )
    return (proto_grad, feature_grad)


def vmem():
    return pl.BlockSpec(memory_space=pltpu.VMEM)


def smem():
    return pl.BlockSpec(memory_space=pltpu.SMEM)


def swap(x, axis, bit):
    return lax.ppermute(x, axis, [(i, i ^ bit) for i in range(lax.axis_size(axis))])


def fold(parts, op):
    parts = list(parts)
    while len(parts) > 1:
        parts = [op(*parts[k : k + 2]) if k + 1 < len(parts) else parts[k] for k in range(0, len(parts), 2)]
    return parts[0]


def lane_tiles(x):
    return [x[:, k : k + LANES] for k in range(0, x.shape[1], LANES)]


def spread_rows(flat, out_ref):
    for j in range(flat.shape[0]):
        wide = jnp.broadcast_to(flat[j : j + 1, :], (LANES, LANES))
        out_ref[j * LANES : (j + 1) * LANES, :] = wide.T


def gather_rows(acc_ref):
    n = acc_ref.shape[0] // LANES
    rows = [
        jnp.sum(acc_ref[j * LANES : (j + 1) * LANES, :].T, axis=0, keepdims=True) for j in range(n)
    ]
    return jnp.concatenate(rows, axis=0)


def own_body(place_ref, t_ref, s_ref, w_ref, out_ref, scores_ref):
    rows = t_ref.shape[0]
    half = rows // 2
    width = scores_ref.shape[2]
    count = scores_ref.shape[0]
    t = t_ref[...]
    s = s_ref[...]

    def scores(j, so_far):
        w = w_ref[:, pl.ds(pl.multiple_of(j * width, width), width)]
        a = jnp.dot(t, w, preferred_element_type=jnp.float32)
        b = jnp.dot(s, w, preferred_element_type=jnp.float32)
        scores_ref[j] = b
        return (
            jnp.maximum(so_far[0], fold(lane_tiles(a), jnp.maximum)),
            jnp.maximum(so_far[1], fold(lane_tiles(b), jnp.maximum)),
        )

    low = jnp.full((rows, LANES), -jnp.inf, jnp.float32)
    t_max, s_max = lax.fori_loop(0, count, scores, (low, low))
    s_col = jnp.max(s_max, axis=1, keepdims=True)

    def total(j, so_far):
        e = jnp.exp2((scores_ref[j] - s_col) * S_EXP)
        return so_far + fold(lane_tiles(e), jnp.add)

    s_sum = lax.fori_loop(0, count, total, jnp.zeros((rows, LANES), jnp.float32))
    first = pl.multiple_of(place_ref[0] * half, half)
    out_ref[0:half, :] = t_ref[pl.ds(first, half), :].astype(jnp.float32)
    out_ref[half : 2 * half, :] = s_ref[pl.ds(first, half), :].astype(jnp.float32)
    stats = [
        jnp.max(t_max.T, axis=0, keepdims=True),
        jnp.max(s_max.T, axis=0, keepdims=True),
        jnp.sum(s_sum.T, axis=0, keepdims=True),
        jnp.zeros((STAT_ROWS - 3, LANES), jnp.float32),
    ]
    out_ref[2 * half :, :] = jnp.concatenate(stats, axis=0)


def exp_body(place_ref, mine_ref, other_ref, w_ref, *refs):
    k_refs = refs[:PARTS]
    s_ref, t_scr, m_scr = refs[PARTS:]
    blocks = mine_ref.shape[0]
    rows = LANES
    half = rows // 2
    core = place_ref[0]
    for j in range(blocks):
        a = pl.multiple_of(j * rows + core * half, half)
        b = pl.multiple_of(j * rows + (1 - core) * half, half)
        t_scr[pl.ds(a, half), :] = mine_ref[j, 0:half, :].astype(jnp.bfloat16)
        t_scr[pl.ds(b, half), :] = other_ref[j, 0:half, :].astype(jnp.bfloat16)
        s_ref[pl.ds(a, half), :] = mine_ref[j, half : 2 * half, :].astype(jnp.bfloat16)
        s_ref[pl.ds(b, half), :] = other_ref[j, half : 2 * half, :].astype(jnp.bfloat16)
        wide = jnp.broadcast_to(mine_ref[j, 2 * half : 2 * half + 1, :], (LANES, LANES))
        m_scr[j * rows : (j + 1) * rows, :] = wide.T
    t = t_scr[...]
    m = m_scr[:, 0:1]
    per, unused, width = k_refs[0].shape
    for p in range(PARTS):

        def block(j, unused, p=p):
            start = pl.multiple_of((p * per + j) * width, width)
            s = jnp.dot(t, w_ref[:, pl.ds(start, width)], preferred_element_type=jnp.float32)
            k_refs[p][j] = jnp.exp2((s - m) * T_EXP)
            return 0

        lax.fori_loop(0, per, block, 0)


def sweep_body(first, n_in, *refs):
    k_refs = refs[:PARTS]
    in_refs = refs[PARTS : PARTS + n_in]
    rest = refs[PARTS + n_in :]
    if first:
        out_refs, rest = rest[:PARTS], rest[PARTS:]
    else:
        out_refs = k_refs
    o_ref, c_ref, r_scr, acc_ref = rest
    if first:
        peak = fold([x[0] for x in in_refs], jnp.maximum)
        scale = jnp.exp2((in_refs[0][0] - peak) * T_EXP)
    else:
        scale = 1.0 / fold([x[...] for x in in_refs], jnp.add)
    spread_rows(scale, r_scr)
    acc_ref[...] = jnp.zeros_like(acc_ref)
    per, rows, width = k_refs[0].shape
    tiles = width // LANES
    unroll = 32
    steps = rows // SUB // unroll

    for p in range(PARTS):
        k_ref, out_ref = k_refs[p], out_refs[p]

        def block(j, unused, p=p, k_ref=k_ref, out_ref=out_ref):
            def down(i, sums):
                base = pl.multiple_of(i * (unroll * SUB), unroll * SUB)
                for u in range(unroll):
                    at = pl.ds(base + u * SUB, SUB)
                    rb = r_scr[at, :]
                    new = []
                    for q in range(tiles):
                        x = k_ref[j, at, q * LANES : (q + 1) * LANES] * rb
                        if first:
                            out_ref[j, at, q * LANES : (q + 1) * LANES] = x
                        new.append(sums[q] + x)
                    sums = tuple(new)
                return sums

            zero = jnp.zeros((SUB, LANES), jnp.float32)
            sums = lax.fori_loop(0, steps, down, (zero,) * tiles)
            cols = [1.0 / jnp.sum(x, axis=0, keepdims=True) for x in sums]
            for q in range(tiles):
                c_ref[p * per + j, :, q * LANES : (q + 1) * LANES] = cols[q]
            wide = [jnp.broadcast_to(x, (SUB, LANES)) for x in cols]

            def across(i, unused):
                base = pl.multiple_of(i * (unroll * SUB), unroll * SUB)
                for u in range(unroll):
                    at = pl.ds(base + u * SUB, SUB)
                    x = [out_ref[j, at, q * LANES : (q + 1) * LANES] * wide[q] for q in range(tiles)]
                    acc_ref[at, :] = acc_ref[at, :] + fold(x, jnp.add)
                return 0

            lax.fori_loop(0, steps, across, 0)
            return 0

        lax.fori_loop(0, per, block, 0)
    o_ref[...] = gather_rows(acc_ref)


def student_scale(stat_refs):
    peak = fold([x[1] for x in stat_refs], jnp.maximum)
    total = fold([x[2] * jnp.exp2((x[1] - peak) * S_EXP) for x in stat_refs], jnp.add)
    return peak, 1.0 / (total * student_temp)


def final_body(n_in, own_only, *refs):
    k_refs = refs[:PARTS]
    row_refs = refs[PARTS : PARTS + n_in]
    stat_refs = refs[PARTS + n_in : PARTS + 2 * n_in]
    rest = refs[PARTS + 2 * n_in :]
    if own_only:
        c_ref, s_ref, w_ref, out_ref, r_scr, m_scr, i_scr = rest
    else:
        c_ref, s_ref, w_ref, place_ref, out_ref, r_scr, m_scr, i_scr = rest
    rows = r_scr.shape[0]
    n = rows // LANES
    row_scale = 1.0 / fold([x[...] for x in row_refs], jnp.add)
    peak, inverse = student_scale(stat_refs)
    spread_rows((row_scale * (1.0 / student_temp))[:n], r_scr)
    spread_rows(peak[:n], m_scr)
    spread_rows(inverse[:n], i_scr)
    per, unused, width = k_refs[0].shape
    s = s_ref[0:rows, :]
    m = m_scr[:, 0:1]
    inv = i_scr[:, 0:1]
    r = r_scr[:, 0:1]
    if own_only:
        out_ref[...] = jnp.zeros_like(out_ref)
    else:
        shape = (out_ref.shape[0], s.shape[1])
        wanted = lax.broadcasted_iota(jnp.int32, shape, 0) + place_ref[1] * shape[0]
        pick = (lax.broadcasted_iota(jnp.int32, shape, 1) == wanted).astype(jnp.float32)
        picked = lax.dot_general(
            pick.astype(jnp.bfloat16), s, (((1,), (1,)), ((), ())), preferred_element_type=jnp.float32
        ).astype(jnp.bfloat16)
    for p in range(PARTS):

        def block(j, unused, p=p):
            start = pl.multiple_of((p * per + j) * width, width)
            w = w_ref[:, pl.ds(start, width)]
            scores = jnp.dot(s, w, preferred_element_type=jnp.float32)
            probs = jnp.exp2((scores - m) * S_EXP) * inv
            target = k_refs[p][j, 0:rows, :] * r * c_ref[p * per + j]
            grad = (probs - target).astype(jnp.bfloat16)
            if own_only:
                out_ref[...] += lax.dot_general(
                    grad, w, (((1,), (1,)), ((), ())), preferred_element_type=jnp.float32
                )
            else:
                out_ref[:, pl.ds(start, width)] = jnp.dot(
                    picked, grad, preferred_element_type=jnp.float32
                )
            return 0

        lax.fori_loop(0, per, block, 0)


def all_crops(teacher_feat, student_feat, proto_weight):
    own, depth = teacher_feat.shape
    n_dp = lax.axis_size("dp")
    n_proto = lax.axis_size("proto")
    rows = own * n_dp
    cols = proto_weight.shape[1]
    width = 1024
    per = cols // width // PARTS
    f32 = jnp.float32
    params = pltpu.CompilerParams(vmem_limit_bytes=16 << 20)
    place = jnp.stack([lax.axis_index("proto") % 2, lax.axis_index("dp")]).astype(jnp.int32)

    payload = pl.pallas_call(
        own_body,
        out_shape=jax.ShapeDtypeStruct((own + STAT_ROWS, depth), f32),
        in_specs=[smem(), vmem(), vmem(), vmem()],
        out_specs=vmem(),
        scratch_shapes=[pltpu.VMEM((cols // width, own, width), f32)],
        compiler_params=params,
        name="own_stats",
    )(place, teacher_feat, student_feat, proto_weight)

    mine = payload[None]
    bit = 1
    while bit < n_dp:
        mine = jnp.concatenate([mine, swap(mine, "dp", bit)], axis=0)
        bit *= 2
    other = swap(mine, "proto", 1)
    stats = jnp.swapaxes(mine[:, own : own + 3, :], 0, 1)

    def everyone(x):
        return [x] + [swap(x, "proto", k) for k in range(1, n_proto)]

    all_stats = everyone(stats)
    k_shape = pltpu.VMEM((per, rows, width), f32)
    *kernel, s_all = pl.pallas_call(
        exp_body,
        out_shape=(k_shape,) * PARTS + (jax.ShapeDtypeStruct((rows, depth), jnp.bfloat16),),
        in_specs=[smem(), vmem(), vmem(), vmem()],
        out_specs=(vmem(),) * (PARTS + 1),
        scratch_shapes=[pltpu.VMEM((rows, depth), jnp.bfloat16), pltpu.VMEM((rows, LANES), f32)],
        compiler_params=params,
        name="kernel_exp",
    )(place, mine, other, proto_weight)

    def sweep(kernel, ins, first):
        outs = (
            jax.ShapeDtypeStruct((rows // LANES, LANES), f32),
            jax.ShapeDtypeStruct((cols // width, 1, width), f32),
        )
        kept = (k_shape,) * PARTS if first else ()
        result = pl.pallas_call(
            lambda *refs: sweep_body(first, len(ins), *refs),
            out_shape=kept + outs,
            in_specs=[vmem()] * (PARTS + len(ins)),
            out_specs=(vmem(),) * (len(kept) + 2),
            scratch_shapes=[pltpu.VMEM((rows, LANES), f32), pltpu.VMEM((rows, LANES), f32)],
            input_output_aliases={k: k for k in range(len(kept))},
            compiler_params=params,
            name="sweep_first" if first else "sweep",
        )(*kernel, *ins)
        return (result[:PARTS] if first else kernel), result[-2], result[-1]

    ins = all_stats
    for it in range(ITERS):
        kernel, row_part, col_scale = sweep(kernel, ins, it == 0)
        ins = everyone(row_part)

    def final(own_only, extra, shape, crops, name):
        return pl.pallas_call(
            lambda *refs: final_body(len(ins), own_only, *refs),
            out_shape=jax.ShapeDtypeStruct(shape, f32),
            in_specs=[vmem()] * (PARTS + 2 * len(ins) + 3) + [smem()] * len(extra),
            out_specs=vmem(),
            scratch_shapes=[pltpu.VMEM((crops, LANES), f32)] * 3,
            compiler_params=params,
            name=name,
        )(*kernel, *ins, *all_stats, col_scale, s_all, proto_weight, *extra)

    part = final(True, (), (own, depth), own, "own_grad")
    parts = everyone(part)
    proto_grad = final(False, (place,), (depth // n_dp, cols), rows, "proto_grad")
    feature_grad = fold(parts, jnp.add)
    return (proto_grad, feature_grad)


def solution(mesh):
    n_dp = mesh.shape["dp"]
    n_proto = mesh.shape["proto"]

    def shards(teacher_feat, student_feat, proto_weight):
        own, depth = teacher_feat.shape
        cols = proto_weight.shape[1]
        fits = (
            own * n_dp * cols * 4 <= KERNEL_BYTES
            and own == LANES
            and depth == LANES
            and cols % (PARTS * 1024) == 0
            and n_dp & (n_dp - 1) == 0
            and n_proto & (n_proto - 1) == 0
            and 2 <= n_proto <= 8
            and depth % (n_dp * SUB) == 0
        )
        plan = all_crops if fits else split_crops
        return plan(teacher_feat, student_feat, proto_weight)

    return jax.shard_map(
        shards,
        mesh=mesh,
        in_specs=(P("dp", None), P("dp", None), P(None, "proto")),
        out_specs=(P("dp", "proto"), P("dp", None)),
        check_vma=False,
    )
```

```python
import math

import jax
import jax.numpy as jnp
from jax import lax
from jax.experimental import pallas as pl
from jax.experimental.pallas import tpu as pltpu
from jax.sharding import PartitionSpec as P

ITERS = 3

teacher_temp = 0.07
student_temp = 0.1

LOG2E = math.log2(math.e)
T_EXP = LOG2E / teacher_temp
S_EXP = LOG2E / student_temp

LANES = 128
SUB = 8
PARTS = 4
STAT_ROWS = 8
KERNEL_BYTES = 32 << 20


def combined_all(value, axis, combine):
    everything = jax.tree.map(lambda part: lax.all_gather(part, axis), value)
    leading = jax.tree.map(lambda part: part[0], everything)

    def step(k, so_far):
        return combine(so_far, jax.tree.map(lambda part: part[k], everything))

    return lax.fori_loop(1, lax.axis_size(axis), step, leading)


def divided_logits(features, prototypes, divisor):
    return jnp.dot(features, prototypes, preferred_element_type=jnp.float32) / divisor


def combine_stats(earlier, later):
    teacher_peak = jnp.maximum(earlier[0], later[0])
    student_peak = jnp.maximum(earlier[1], later[1])
    merged_total = earlier[2] * jnp.exp(earlier[1] - student_peak) + later[2] * jnp.exp(
        later[1] - student_peak
    )
    return (teacher_peak, student_peak, merged_total)


def split_crops(teacher_feat, student_feat, proto_weight):
    teacher_scores = divided_logits(teacher_feat, proto_weight, teacher_temp)
    student_scores = divided_logits(student_feat, proto_weight, student_temp)
    local_teacher = jnp.max(teacher_scores, axis=1)
    local_student = jnp.max(student_scores, axis=1)
    local_total = jnp.sum(jnp.exp(student_scores - local_student[:, None]), axis=1)
    teacher_peak, student_peak, student_total = combined_all(
        (local_teacher, local_student, local_total), "proto", combine_stats
    )
    kernel = jnp.exp(teacher_scores - teacher_peak[:, None])
    row_scale = jnp.ones((teacher_feat.shape[0],), jnp.float32)
    for sweep in range(ITERS):
        col_part = jnp.sum(kernel * row_scale[:, None], axis=0)
        col_scale = 1.0 / lax.psum(col_part, "dp")
        row_part = jnp.sum(kernel * col_scale[None, :], axis=1)
        row_scale = 1.0 / lax.psum(row_part, "proto")
    target = kernel * row_scale[:, None] * col_scale[None, :]
    student_probs = jnp.exp(student_scores - student_peak[:, None]) / student_total[:, None]
    grad_scores = ((student_probs - target) / student_temp).astype(jnp.bfloat16)
    input_part = lax.dot_general(
        grad_scores, proto_weight, (((1,), (1,)), ((), ())), preferred_element_type=jnp.float32
    )
    feature_grad = lax.psum(input_part, "proto")
    proto_grad = lax.psum_scatter(
        lax.dot_general(
            student_feat, grad_scores, (((0,), (0,)), ((), ())), preferred_element_type=jnp.float32
        ),
        "dp",
        scatter_dimension=0,
        tiled=True,
    )
    return (proto_grad, feature_grad)


def vmem():
    return pl.BlockSpec(memory_space=pltpu.VMEM)


def smem():
    return pl.BlockSpec(memory_space=pltpu.SMEM)


def swap(x, axis, bit):
    return lax.ppermute(x, axis, [(i, i ^ bit) for i in range(lax.axis_size(axis))])


def fold(parts, op):
    parts = list(parts)
    while len(parts) > 1:
        parts = [op(*parts[k : k + 2]) if k + 1 < len(parts) else parts[k] for k in range(0, len(parts), 2)]
    return parts[0]


def lane_tiles(x):
    return [x[:, k : k + LANES] for k in range(0, x.shape[1], LANES)]


def spread_rows(flat, out_ref):
    for j in range(flat.shape[0]):
        wide = jnp.broadcast_to(flat[j : j + 1, :], (LANES, LANES))
        out_ref[j * LANES : (j + 1) * LANES, :] = wide.T


def gather_rows(acc_ref):
    n = acc_ref.shape[0] // LANES
    rows = [
        jnp.sum(acc_ref[j * LANES : (j + 1) * LANES, :].T, axis=0, keepdims=True) for j in range(n)
    ]
    return jnp.concatenate(rows, axis=0)


def row_max(acc):
    return [
        jnp.max(acc[k : k + LANES, :].T, axis=0, keepdims=True) for k in range(0, acc.shape[0], LANES)
    ]


def own_body(place_ref, s_ref, w_hbm, out_ref, w_ref, scores_ref, sems):
    rows = s_ref.shape[0]
    half = rows // 2
    count, unused, width = scores_ref.shape
    copies = []
    for j in range(count):
        at = pl.ds(j * width, width)
        copies.append(pltpu.make_async_copy(w_hbm.at[:, at], w_ref.at[:, at], sems.at[j]))
        copies[-1].start()
    s = s_ref[...]
    s_max = None
    for j in range(count):
        copies[j].wait()
        b = jnp.dot(s, w_ref[:, j * width : (j + 1) * width], preferred_element_type=jnp.float32)
        scores_ref[j] = b
        top = fold(lane_tiles(b), jnp.maximum)
        s_max = top if s_max is None else jnp.maximum(s_max, top)
    s_col = jnp.broadcast_to(jnp.max(s_max, axis=1, keepdims=True), (rows, LANES))

    def total(j, so_far):
        e = [jnp.exp2((x - s_col) * S_EXP) for x in lane_tiles(scores_ref[j])]
        return so_far + fold(e, jnp.add)

    s_sum = lax.fori_loop(0, count, total, jnp.zeros((rows, LANES), jnp.float32))
    first = pl.multiple_of(place_ref[0] * half, half)
    out_ref[0:half, :] = s_ref[pl.ds(first, half), :].astype(jnp.float32)
    stats = [
        jnp.max(s_max.T, axis=0, keepdims=True),
        jnp.sum(s_sum.T, axis=0, keepdims=True),
        jnp.zeros((STAT_ROWS - 2, LANES), jnp.float32),
    ]
    out_ref[half:, :] = jnp.concatenate(stats, axis=0)


def join_halves(core, mine, other, out_ref, first):
    half = LANES // 2
    for j in range(mine.shape[0]):
        base = (first + j) * LANES
        a = pl.multiple_of(base + core * half, half)
        b = pl.multiple_of(base + (1 - core) * half, half)
        out_ref[pl.ds(a, half), :] = mine[j, 0:half, :].astype(jnp.bfloat16)
        out_ref[pl.ds(b, half), :] = other[j, 0:half, :].astype(jnp.bfloat16)


def scores_body(place_ref, mine_ref, other_ref, w_ref, *refs):
    k_refs = refs[:PARTS]
    max_ref, t_scr, acc_ref = refs[PARTS:]
    join_halves(place_ref[0], mine_ref, other_ref, t_scr, 0)
    t = t_scr[...]
    per, unused, width = k_refs[0].shape
    acc_ref[...] = jnp.full(acc_ref.shape, -jnp.inf, jnp.float32)
    for p in range(PARTS):

        def block(j, unused, p=p):
            start = pl.multiple_of((p * per + j) * width, width)
            s = jnp.dot(t, w_ref[:, pl.ds(start, width)], preferred_element_type=jnp.float32) * T_EXP
            k_refs[p][j] = s
            acc_ref[...] = jnp.maximum(acc_ref[...], fold(lane_tiles(s), jnp.maximum))
            return 0

        lax.fori_loop(0, per, block, 0)
    max_ref[...] = jnp.concatenate(row_max(acc_ref), axis=0)


def sweep_body(first, n_in, n_extra, *refs):
    k_refs, refs = refs[:PARTS], refs[PARTS:]
    in_refs, refs = refs[:n_in], refs[n_in:]
    extra_refs, refs = refs[:n_extra], refs[n_extra:]
    if first:
        k_refs, refs = refs[:PARTS], refs[PARTS:]
    o_ref, c_ref, r_scr, acc_ref = refs
    per, rows, width = k_refs[0].shape
    n = rows // LANES
    if first:
        spread_rows(fold([x[...] for x in in_refs], jnp.maximum), r_scr)
    else:
        spread_rows(1.0 / fold([x[0:n, :] for x in in_refs], jnp.add), r_scr)
    acc_ref[...] = jnp.zeros_like(acc_ref)
    tiles = width // LANES
    unroll = 32
    steps = rows // SUB // unroll

    for p in range(PARTS):
        k_ref = k_refs[p]

        def block(j, unused, p=p, k_ref=k_ref):
            def down(i, sums):
                base = pl.multiple_of(i * (unroll * SUB), unroll * SUB)
                for u in range(unroll):
                    at = pl.ds(base + u * SUB, SUB)
                    rb = r_scr[at, :]
                    new = []
                    for q in range(tiles):
                        x = k_ref[j, at, q * LANES : (q + 1) * LANES]
                        if first:
                            x = jnp.exp2(x - rb)
                            k_ref[j, at, q * LANES : (q + 1) * LANES] = x
                        else:
                            x = x * rb
                        new.append(sums[q] + x)
                    sums = tuple(new)
                return sums

            zero = jnp.zeros((SUB, LANES), jnp.float32)
            sums = lax.fori_loop(0, steps, down, (zero,) * tiles)
            cols = [1.0 / jnp.sum(x, axis=0, keepdims=True) for x in sums]
            for q in range(tiles):
                c_ref[p * per + j, :, q * LANES : (q + 1) * LANES] = cols[q]
            wide = [jnp.broadcast_to(x, (SUB, LANES)) for x in cols]

            def across(i, unused):
                base = pl.multiple_of(i * (unroll * SUB), unroll * SUB)
                for u in range(unroll):
                    at = pl.ds(base + u * SUB, SUB)
                    x = [k_ref[j, at, q * LANES : (q + 1) * LANES] * wide[q] for q in range(tiles)]
                    acc_ref[at, :] = acc_ref[at, :] + fold(x, jnp.add)
                return 0

            lax.fori_loop(0, steps, across, 0)
            return 0

        lax.fori_loop(0, per, block, 0)
    o_ref[0:n, :] = gather_rows(acc_ref)
    if n_extra:
        half = LANES // 2
        for k in range(2):
            rows_k = [x[j, half + k : half + k + 1, :] for x in extra_refs for j in range(x.shape[0])]
            o_ref[(k + 1) * n : (k + 2) * n, :] = jnp.concatenate(rows_k, axis=0)


def grad_tiles(k_ref, j, first, last, c_row, s_scr, g_scr, r_scr, b_scr, rows):
    tiles = (last - first) // LANES
    step = 2 * SUB
    c = [jnp.broadcast_to(c_row[:, q * LANES : (q + 1) * LANES], (step, LANES)) for q in range(tiles)]
    for i in range(0, rows, step):
        at = slice(i, i + step)
        rb, bb = r_scr[at, :], b_scr[at, :]
        for q in range(tiles):
            lanes = slice(q * LANES, (q + 1) * LANES)
            probs = jnp.exp2(s_scr[at, lanes] * S_EXP - bb)
            k = k_ref[j, at, first + q * LANES : first + (q + 1) * LANES]
            g_scr[at, lanes] = (probs - k * rb * c[q]).astype(jnp.bfloat16)


def final_body(n_in, own_only, *refs):
    k_refs, refs = refs[:PARTS], refs[PARTS:]
    row_refs, refs = refs[:n_in], refs[n_in:]
    stat_refs, refs = refs[:n_in], refs[n_in:]
    near_ref, near_other_ref, far_ref, far_other_ref, c_ref, w_ref, place_ref, out_ref = refs[:8]
    f_scr, r_scr, b_scr, *pairs = refs[8:]
    rows = r_scr.shape[0]
    used = rows // LANES
    n = stat_refs[0].shape[0] // 3
    row_scale = 1.0 / fold([x[...] for x in row_refs], jnp.add)
    peak = fold([x[n : 2 * n, :] for x in stat_refs], jnp.maximum)
    total = fold(
        [x[2 * n :, :] * jnp.exp2((x[n : 2 * n, :] - peak) * S_EXP) for x in stat_refs], jnp.add
    )
    shift = peak * S_EXP + jnp.log(total * student_temp) * LOG2E
    spread_rows((row_scale * (1.0 / student_temp))[:used], r_scr)
    spread_rows(shift[:used], b_scr)
    core = place_ref[0]
    if own_only:
        join_halves(core, near_ref.at[0:1], near_other_ref.at[0:1], f_scr, 0)
        out_ref[...] = jnp.zeros_like(out_ref)
    else:
        join_halves(core, near_ref, near_other_ref, f_scr, 0)
        join_halves(core, far_ref, far_other_ref, f_scr, near_ref.shape[0])
    s = f_scr[...]
    if not own_only:
        shape = (out_ref.shape[0], s.shape[1])
        wanted = lax.broadcasted_iota(jnp.int32, shape, 0) + place_ref[1] * shape[0]
        pick = (lax.broadcasted_iota(jnp.int32, shape, 1) == wanted).astype(jnp.float32)
        picked = lax.dot_general(
            pick.astype(jnp.bfloat16), s, (((1,), (1,)), ((), ())), preferred_element_type=jnp.float32
        ).astype(jnp.bfloat16)
    per, unused, width = k_refs[0].shape
    tile = pairs[0].shape[1]
    for p in range(PARTS):

        def block(j, unused, p=p):
            start = pl.multiple_of((p * per + j) * width, width)
            for q in range(width // tile):
                s_scr, g_scr = pairs[2 * (q % (len(pairs) // 2)) :][:2]
                at = pl.ds(start + q * tile, tile)
                w = w_ref[:, at]
                s_scr[...] = jnp.dot(s, w, preferred_element_type=jnp.float32)
                c_row = c_ref[p * per + j, :, q * tile : (q + 1) * tile]
                grad_tiles(
                    k_refs[p], j, q * tile, (q + 1) * tile, c_row, s_scr, g_scr, r_scr, b_scr, rows
                )
                if own_only:
                    out_ref[...] += lax.dot_general(
                        g_scr[...], w, (((1,), (1,)), ((), ())), preferred_element_type=jnp.float32
                    )
                else:
                    out_ref[:, at] = jnp.dot(picked, g_scr[...], preferred_element_type=jnp.float32)
            return 0

        lax.fori_loop(0, per, block, 0)


def all_crops(teacher_feat, student_feat, proto_weight):
    own, depth = teacher_feat.shape
    n_dp = lax.axis_size("dp")
    n_proto = lax.axis_size("proto")
    rows = own * n_dp
    n = rows // LANES
    cols = proto_weight.shape[1]
    width = 1024
    per = cols // width // PARTS
    half = own // 2
    f32 = jnp.float32
    params = pltpu.CompilerParams(vmem_limit_bytes=16 << 20)
    place = jnp.stack([lax.axis_index("proto") % 2, lax.axis_index("dp")]).astype(jnp.int32)

    def everyone(x):
        return [x] + [swap(x, "proto", k) for k in range(1, n_proto)]

    def spread(x, bits):
        for bit in bits:
            x = jnp.concatenate([x, swap(x, "dp", bit)], axis=0)
        return x

    bits = [1 << k for k in range(n_dp.bit_length() - 1)][::-1]
    teacher_half = lax.dynamic_slice_in_dim(teacher_feat, place[0] * half, half, 0).astype(f32)
    mine = spread(teacher_half[None], bits)
    other = swap(mine, "proto", 1)

    chunk = 1024
    student_part, weight = pl.pallas_call(
        own_body,
        out_shape=(
            jax.ShapeDtypeStruct((half + STAT_ROWS, depth), f32),
            pltpu.VMEM(proto_weight.shape, proto_weight.dtype),
        ),
        in_specs=[smem(), vmem(), pl.BlockSpec(memory_space=pl.ANY)],
        out_specs=(vmem(), vmem()),
        scratch_shapes=[
            pltpu.VMEM((cols // chunk, own, chunk), f32),
            pltpu.SemaphoreType.DMA((cols // chunk,)),
        ],
        compiler_params=params,
        name="own_stats",
    )(place, student_feat, proto_weight)
    near = spread(student_part[None], bits[:-1])

    k_shape = pltpu.VMEM((per, rows, width), f32)
    flat = jax.ShapeDtypeStruct((n, LANES), f32)
    *kernel, local_peak = pl.pallas_call(
        scores_body,
        out_shape=(k_shape,) * PARTS + (flat,),
        in_specs=[smem(), vmem(), vmem(), vmem()],
        out_specs=(vmem(),) * (PARTS + 1),
        scratch_shapes=[pltpu.VMEM((rows, depth), jnp.bfloat16), pltpu.VMEM((rows, LANES), f32)],
        compiler_params=params,
        name="scores",
    )(place, mine, other, weight)

    def sweep(kernel, ins, extra, first):
        outs = (
            jax.ShapeDtypeStruct((3 * n if extra else n, LANES), f32),
            jax.ShapeDtypeStruct((cols // width, 1, width), f32),
        )
        kept = (k_shape,) * PARTS if first else ()
        result = pl.pallas_call(
            lambda *refs: sweep_body(first, len(ins), len(extra), *refs),
            out_shape=kept + outs,
            in_specs=[vmem()] * (PARTS + len(ins) + len(extra)),
            out_specs=(vmem(),) * (len(kept) + 2),
            scratch_shapes=[pltpu.VMEM((rows, LANES), f32), pltpu.VMEM((rows, LANES), f32)],
            input_output_aliases={k: k for k in range(len(kept))},
            compiler_params=params,
            name="sweep_first" if first else "sweep",
        )(*kernel, *ins, *extra)
        return (result[:PARTS] if first else kernel), result[-2], result[-1]

    ins = everyone(local_peak)
    far = swap(near, "dp", bits[-1])
    near_other = swap(near, "proto", 1)
    far_other = swap(far, "proto", 1)
    stats = None
    for it in range(ITERS):
        extra = (near, far) if it == ITERS - 2 else ()
        kernel, row_part, col_scale = sweep(kernel, ins, extra, it == 0)
        ins = everyone(row_part)
        if extra:
            stats = ins

    def final(own_only, shape, crops, tile, name):
        scratch = [pltpu.VMEM((crops, depth), jnp.bfloat16)] + [pltpu.VMEM((crops, LANES), f32)] * 2
        for unused in range(4):
            scratch += [pltpu.VMEM((crops, tile), f32), pltpu.VMEM((crops, tile), jnp.bfloat16)]
        return pl.pallas_call(
            lambda *refs: final_body(len(ins), own_only, *refs),
            out_shape=jax.ShapeDtypeStruct(shape, f32),
            in_specs=[vmem()] * (PARTS + 2 * len(ins) + 6) + [smem()],
            out_specs=vmem(),
            scratch_shapes=scratch,
            compiler_params=params,
            name=name,
        )(*kernel, *ins, *stats, near, near_other, far, far_other, col_scale, weight, place)

    parts = everyone(final(True, (own, depth), own, 256, "own_grad"))
    proto_grad = final(False, (depth // n_dp, cols), rows, 256, "proto_grad")
    feature_grad = fold(parts, jnp.add)
    return (proto_grad, feature_grad)


def solution(mesh):
    n_dp = mesh.shape["dp"]
    n_proto = mesh.shape["proto"]

    def shards(teacher_feat, student_feat, proto_weight):
        own, depth = teacher_feat.shape
        cols = proto_weight.shape[1]
        fits = (
            own * n_dp * cols * 4 <= KERNEL_BYTES
            and own == LANES
            and depth == LANES
            and cols % (PARTS * 1024) == 0
            and n_dp & (n_dp - 1) == 0
            and n_proto & (n_proto - 1) == 0
            and 2 <= n_proto <= 8
            and depth % (n_dp * SUB) == 0
        )
        plan = all_crops if fits else split_crops
        return plan(teacher_feat, student_feat, proto_weight)

    return jax.shard_map(
        shards,
        mesh=mesh,
        in_specs=(P("dp", None), P("dp", None), P(None, "proto")),
        out_specs=(P("dp", "proto"), P("dp", None)),
        check_vma=False,
    )
```

```python
import math

import jax
import jax.numpy as jnp
from jax import lax
from jax.experimental import pallas as pl
from jax.experimental.pallas import tpu as pltpu
from jax.sharding import PartitionSpec as P

ITERS = 3

teacher_temp = 0.07
student_temp = 0.1

LOG2E = math.log2(math.e)
T_EXP = LOG2E / teacher_temp
S_EXP = LOG2E / student_temp

LANES = 128
SUB = 8
PARTS = 4
STAT_ROWS = 8
KERNEL_BYTES = 32 << 20


def combined_all(value, axis, combine):
    everything = jax.tree.map(lambda part: lax.all_gather(part, axis), value)
    leading = jax.tree.map(lambda part: part[0], everything)

    def step(k, so_far):
        return combine(so_far, jax.tree.map(lambda part: part[k], everything))

    return lax.fori_loop(1, lax.axis_size(axis), step, leading)


def divided_logits(features, prototypes, divisor):
    return jnp.dot(features, prototypes, preferred_element_type=jnp.float32) / divisor


def combine_stats(earlier, later):
    teacher_peak = jnp.maximum(earlier[0], later[0])
    student_peak = jnp.maximum(earlier[1], later[1])
    merged_total = earlier[2] * jnp.exp(earlier[1] - student_peak) + later[2] * jnp.exp(
        later[1] - student_peak
    )
    return (teacher_peak, student_peak, merged_total)


def split_crops(teacher_feat, student_feat, proto_weight):
    teacher_scores = divided_logits(teacher_feat, proto_weight, teacher_temp)
    student_scores = divided_logits(student_feat, proto_weight, student_temp)
    local_teacher = jnp.max(teacher_scores, axis=1)
    local_student = jnp.max(student_scores, axis=1)
    local_total = jnp.sum(jnp.exp(student_scores - local_student[:, None]), axis=1)
    teacher_peak, student_peak, student_total = combined_all(
        (local_teacher, local_student, local_total), "proto", combine_stats
    )
    kernel = jnp.exp(teacher_scores - teacher_peak[:, None])
    row_scale = jnp.ones((teacher_feat.shape[0],), jnp.float32)
    for sweep in range(ITERS):
        col_part = jnp.sum(kernel * row_scale[:, None], axis=0)
        col_scale = 1.0 / lax.psum(col_part, "dp")
        row_part = jnp.sum(kernel * col_scale[None, :], axis=1)
        row_scale = 1.0 / lax.psum(row_part, "proto")
    target = kernel * row_scale[:, None] * col_scale[None, :]
    student_probs = jnp.exp(student_scores - student_peak[:, None]) / student_total[:, None]
    grad_scores = ((student_probs - target) / student_temp).astype(jnp.bfloat16)
    input_part = lax.dot_general(
        grad_scores, proto_weight, (((1,), (1,)), ((), ())), preferred_element_type=jnp.float32
    )
    feature_grad = lax.psum(input_part, "proto")
    proto_grad = lax.psum_scatter(
        lax.dot_general(
            student_feat, grad_scores, (((0,), (0,)), ((), ())), preferred_element_type=jnp.float32
        ),
        "dp",
        scatter_dimension=0,
        tiled=True,
    )
    return (proto_grad, feature_grad)


def vmem():
    return pl.BlockSpec(memory_space=pltpu.VMEM)


def smem():
    return pl.BlockSpec(memory_space=pltpu.SMEM)


def swap(x, axis, bit):
    return lax.ppermute(x, axis, [(i, i ^ bit) for i in range(lax.axis_size(axis))])


def fold(parts, op):
    parts = list(parts)
    while len(parts) > 1:
        parts = [op(*parts[k : k + 2]) if k + 1 < len(parts) else parts[k] for k in range(0, len(parts), 2)]
    return parts[0]


NT = (((1,), (1,)), ((), ()))
TN = (((0,), (0,)), ((), ()))


def fold_rows(x, op):
    return fold([x[k : k + SUB, :] for k in range(0, x.shape[0], SUB)], op)


def lane_rows(flat):
    return [jnp.broadcast_to(flat[q : q + 1, :], (SUB, LANES)) for q in range(flat.shape[0])]


def own_body(place_ref, s_ref, w_ref, out_ref, wt_ref, scores_ref):
    rows = s_ref.shape[0]
    half = rows // 2
    count, width, unused = scores_ref.shape
    s = s_ref[...]
    top = None
    for j in range(count):
        wt = w_ref[:, j * width : (j + 1) * width].astype(jnp.float32).T.astype(jnp.bfloat16)
        wt_ref[j * width : (j + 1) * width, :] = wt
        scores = lax.dot_general(wt, s, NT, preferred_element_type=jnp.float32)
        scores_ref[j] = scores
        new = fold_rows(scores, jnp.maximum)
        top = new if top is None else jnp.maximum(top, new)
    peak = jnp.max(top, axis=0, keepdims=True)

    def total(j, so_far):
        return so_far + fold_rows(jnp.exp2((scores_ref[j] - peak) * S_EXP), jnp.add)

    sums = lax.fori_loop(0, count, total, jnp.zeros((SUB, rows), jnp.float32))
    first = pl.multiple_of(place_ref[0] * half, half)
    out_ref[0:half, :] = s_ref[pl.ds(first, half), :].astype(jnp.float32)
    stats = [
        peak,
        jnp.sum(sums, axis=0, keepdims=True),
        jnp.zeros((STAT_ROWS - 2, LANES), jnp.float32),
    ]
    out_ref[half:, :] = jnp.concatenate(stats, axis=0)


def join_halves(core, mine, other, out_ref, first):
    half = LANES // 2
    for j in range(mine.shape[0]):
        base = (first + j) * LANES
        a = pl.multiple_of(base + core * half, half)
        b = pl.multiple_of(base + (1 - core) * half, half)
        out_ref[pl.ds(a, half), :] = mine[j, 0:half, :].astype(jnp.bfloat16)
        out_ref[pl.ds(b, half), :] = other[j, 0:half, :].astype(jnp.bfloat16)


def scores_body(place_ref, mine_ref, other_ref, wt_ref, *refs):
    k_refs = refs[:PARTS]
    max_ref, t_scr, acc_ref = refs[PARTS:]
    join_halves(place_ref[0], mine_ref, other_ref, t_scr, 0)
    t = t_scr[...]
    per = k_refs[0].shape[0]
    chunk = min(per, 1024)
    acc_ref[...] = jnp.full(acc_ref.shape, -jnp.inf, jnp.float32)
    for p in range(PARTS):

        def block(j, unused, p=p):
            at = pl.ds(pl.multiple_of(j * chunk, chunk), chunk)
            w = wt_ref[pl.ds(pl.multiple_of(p * per + j * chunk, chunk), chunk), :]
            s = lax.dot_general(w, t, NT, preferred_element_type=jnp.float32) * T_EXP
            k_refs[p][at, :] = s
            acc_ref[...] = jnp.maximum(acc_ref[...], fold_rows(s, jnp.maximum))
            return 0

        lax.fori_loop(0, per // chunk, block, 0)
    n = max_ref.shape[0]
    tops = [jnp.max(acc_ref[:, q * LANES : (q + 1) * LANES], axis=0, keepdims=True) for q in range(n)]
    max_ref[...] = jnp.concatenate(tops, axis=0)


def sweep_body(first, last, n_in, n_extra, *refs):
    k_refs, refs = refs[:PARTS], refs[PARTS:]
    in_refs, refs = refs[:n_in], refs[n_in:]
    extra_refs, refs = refs[:n_extra], refs[n_extra:]
    if first or last:
        k_refs, refs = refs[:PARTS], refs[PARTS:]
    o_ref = refs[0]
    per, rows = k_refs[0].shape
    n = rows // LANES
    if first:
        scale = fold([x[...] for x in in_refs], jnp.maximum)
    else:
        scale = 1.0 / fold([x[0:n, :] for x in in_refs], jnp.add)
    wide = lane_rows(scale)
    unroll = 16
    group = 2 if last else 4
    chunk = unroll * SUB
    tiles = [slice(q * LANES, (q + 1) * LANES) for q in range(n)]

    def phases(p_down, i_down, p_across, i_across, inverse, acc):
        acc = list(acc)
        new = []

        def load(g):
            out = []
            for u in range(g, g + group):
                at = pl.ds(pl.multiple_of(i_down * chunk, chunk) + u * SUB, SUB)
                x = [k_refs[p_down][at, tiles[q]] for q in range(n)]
                out.append((at, [x[q] - wide[q] if first else x[q] * wide[q] for q in range(n)]))
            return out

        ahead = load(0) if p_down is not None else None
        for g in range(0, unroll, group):
            if p_down is not None:
                now = ahead
                if g + group < unroll and (first or last):
                    ahead = load(g + group)
            if p_across is not None:
                done = []
                for u in range(g, g + group):
                    at = pl.ds(pl.multiple_of(i_across * chunk, chunk) + u * SUB, SUB)
                    for q in range(n):
                        x = k_refs[p_across][at, tiles[q]] * inverse[u]
                        acc[q] = acc[q] + x
                        done.append((at, tiles[q], x))
                if last:
                    for at, lanes, x in done:
                        k_refs[p_across][at, lanes] = x
            if p_down is not None:
                for at, x in now:
                    if first:
                        x = [jnp.exp2(v) for v in x]
                        for q in range(n):
                            k_refs[p_down][at, tiles[q]] = x[q]
                    c = 1.0 / jnp.sum(fold(x, jnp.add), axis=1, keepdims=True)
                    c = jnp.broadcast_to(c, (SUB, LANES))
                    new.append(c)
                if g + group < unroll and not (first or last):
                    ahead = load(g + group)
        return tuple(new), tuple(acc)

    acc = (jnp.zeros((SUB, LANES), jnp.float32),) * n
    inverse = None
    steps = per // chunk
    for p in range(PARTS):
        before = None if p == 0 else p - 1
        inverse, acc = phases(p, 0, before, steps - 1, inverse, acc)

        def step(i, carry, p=p):
            return phases(p, i + 1, p, i, *carry)

        inverse, acc = lax.fori_loop(0, steps - 1, step, (inverse, acc))
    unused, acc = phases(None, 0, PARTS - 1, steps - 1, inverse, acc)
    o_ref[0:n, :] = jnp.concatenate([jnp.sum(x, axis=0, keepdims=True) for x in acc], axis=0)
    if n_extra:
        half = LANES // 2
        for k in range(2):
            rows_k = [x[j, half + k : half + k + 1, :] for x in extra_refs for j in range(x.shape[0])]
            o_ref[(k + 1) * n : (k + 2) * n, :] = jnp.concatenate(rows_k, axis=0)


def final_scales(row_refs, stat_refs):
    n = row_refs[0].shape[0]
    row_scale = 1.0 / fold([x[...] for x in row_refs], jnp.add)
    peak = fold([x[n : 2 * n, :] for x in stat_refs], jnp.maximum)
    total = fold(
        [x[2 * n :, :] * jnp.exp2((x[n : 2 * n, :] - peak) * S_EXP) for x in stat_refs], jnp.add
    )
    shift = peak * S_EXP + jnp.log(total * student_temp) * LOG2E
    return row_scale * (1.0 / student_temp), shift


def grad_rows(k_ref, first, s_scr, g_scr, scale, shift):
    step = 2 * SUB
    scale = [jnp.concatenate([x, x], axis=0) for x in scale]
    shift = [jnp.concatenate([x, x], axis=0) for x in shift]
    for i in range(0, s_scr.shape[0], step):
        for q in range(len(scale)):
            lanes = slice(q * LANES, (q + 1) * LANES)
            probs = jnp.exp2(s_scr[i : i + step, lanes] * S_EXP - shift[q])
            target = k_ref[pl.ds(first + i, step), lanes] * scale[q]
            g_scr[i : i + step, lanes] = (probs - target).astype(jnp.bfloat16)


def own_grad_body(n_in, *refs):
    k_refs, refs = refs[:PARTS], refs[PARTS:]
    row_refs, refs = refs[:n_in], refs[n_in:]
    stat_refs, refs = refs[:n_in], refs[n_in:]
    near_ref, other_ref, wt_ref, place_ref, out_ref, f_scr, *pairs = refs
    scale, shift = final_scales(row_refs, stat_refs)
    scale, shift = lane_rows(scale[0:1]), lane_rows(shift[0:1])
    join_halves(place_ref[0], near_ref.at[0:1], other_ref.at[0:1], f_scr, 0)
    s = f_scr[...]
    per = k_refs[0].shape[0]
    half = len(pairs) // 2
    chunk = pairs[0].shape[0]
    total = jnp.zeros(out_ref.shape, jnp.float32)
    for p in range(PARTS):
        for k in range(per // chunk):
            s_scr, g_scr = pairs[2 * (k % half)], pairs[2 * (k % half) + 1]
            start = p * per + k * chunk
            w = wt_ref[start : start + chunk, :]
            s_scr[...] = lax.dot_general(w, s, NT, preferred_element_type=jnp.float32)
            grad_rows(k_refs[p], k * chunk, s_scr, g_scr, scale, shift)
            total = total + lax.dot_general(g_scr[...], w, TN, preferred_element_type=jnp.float32)
    out_ref[...] = total


def proto_grad_body(n_in, *refs):
    k_refs, refs = refs[:PARTS], refs[PARTS:]
    row_refs, refs = refs[:n_in], refs[n_in:]
    stat_refs, refs = refs[:n_in], refs[n_in:]
    near_ref, near_other_ref, far_ref, far_other_ref, wt_ref, place_ref, out_ref = refs[:7]
    f_scr, s_even, g_even, s_odd, g_odd = refs[7:]
    scale, shift = (lane_rows(x) for x in final_scales(row_refs, stat_refs))
    core = place_ref[0]
    join_halves(core, near_ref, near_other_ref, f_scr, 0)
    join_halves(core, far_ref, far_other_ref, f_scr, near_ref.shape[0])
    s = f_scr[...]
    owned = out_ref.shape[0]
    depth = s.shape[1]
    column = lax.broadcasted_iota(jnp.int32, (depth, LANES), 1)
    wanted = column + place_ref[1] * owned
    pick = (lax.broadcasted_iota(jnp.int32, (depth, LANES), 0) == wanted) & (column < owned)
    pick = pick.astype(jnp.float32).astype(jnp.bfloat16)
    picked = jnp.dot(s, pick, preferred_element_type=jnp.float32).astype(jnp.bfloat16)
    per = k_refs[0].shape[0]
    chunk = s_even.shape[0]
    final_chunk = wt_ref.shape[0] // chunk - 1

    def scores(k, s_scr):
        at = pl.ds(pl.multiple_of(jnp.minimum(k, final_chunk) * chunk, chunk), chunk)
        s_scr[...] = lax.dot_general(wt_ref[at, :], s, NT, preferred_element_type=jnp.float32)

    def finish(k, g_scr):
        at = pl.ds(pl.multiple_of(jnp.maximum(k, 0) * chunk, chunk), chunk)
        part = jnp.dot(g_scr[...], picked, preferred_element_type=jnp.float32)
        out_ref[:, at] = part.T[0:owned, :]

    g_odd[...] = jnp.zeros_like(g_odd)
    scores(0, s_even)
    pairs = per // chunk // 2
    for p in range(PARTS):

        def step(i, unused, p=p):
            k = 2 * (p * pairs + i)
            here = pl.multiple_of(2 * i * chunk, 2 * chunk)
            scores(k + 1, s_odd)
            finish(k - 1, g_odd)
            grad_rows(k_refs[p], here, s_even, g_even, scale, shift)
            scores(k + 2, s_even)
            finish(k, g_even)
            grad_rows(k_refs[p], here + chunk, s_odd, g_odd, scale, shift)
            return 0

        lax.fori_loop(0, pairs, step, 0)
    finish(final_chunk, g_odd)


def all_crops(teacher_feat, student_feat, proto_weight):
    own, depth = teacher_feat.shape
    n_dp = lax.axis_size("dp")
    n_proto = lax.axis_size("proto")
    rows = own * n_dp
    n = rows // LANES
    cols = proto_weight.shape[1]
    per = cols // PARTS
    half = own // 2
    f32 = jnp.float32
    bf16 = jnp.bfloat16

    def grant(mib):
        return pltpu.CompilerParams(vmem_limit_bytes=mib << 20)

    place = jnp.stack([lax.axis_index("proto") % 2, lax.axis_index("dp")]).astype(jnp.int32)

    def everyone(x):
        return [x] + [swap(x, "proto", k) for k in range(1, n_proto)]

    def spread(x, bits):
        for bit in bits:
            x = jnp.concatenate([x, swap(x, "dp", bit)], axis=0)
        return x

    bits = [1 << k for k in range(n_dp.bit_length() - 1)][::-1]
    teacher_half = lax.dynamic_slice_in_dim(teacher_feat, place[0] * half, half, 0).astype(f32)
    mine = spread(teacher_half[None], bits)
    other = swap(mine, "proto", 1)

    chunk = 1024
    student_part, weight_t = pl.pallas_call(
        own_body,
        out_shape=(
            jax.ShapeDtypeStruct((half + STAT_ROWS, depth), f32),
            pltpu.VMEM((cols, depth), bf16),
        ),
        in_specs=[smem(), vmem(), vmem()],
        out_specs=(vmem(),) * 2,
        scratch_shapes=[pltpu.VMEM((cols // chunk, chunk, own), f32)],
        compiler_params=grant(16),
        name="own_stats",
    )(place, student_feat, proto_weight)
    near = spread(student_part[None], bits[:-1])

    k_shape = pltpu.VMEM((per, rows), f32)
    flat = jax.ShapeDtypeStruct((n, LANES), f32)
    *kernel, local_peak = pl.pallas_call(
        scores_body,
        out_shape=(k_shape,) * PARTS + (flat,),
        in_specs=[smem(), vmem(), vmem(), vmem()],
        out_specs=(vmem(),) * (PARTS + 1),
        scratch_shapes=[pltpu.VMEM((rows, depth), bf16), pltpu.VMEM((SUB, rows), f32)],
        compiler_params=grant(16),
        name="scores",
    )(place, mine, other, weight_t)

    def sweep(kernel, ins, extra, it):
        first, last = it == 0, it == ITERS - 1
        kept = (k_shape,) * PARTS if first or last else ()
        outs = (jax.ShapeDtypeStruct((3 * n if extra else n, LANES), f32),)
        result = pl.pallas_call(
            lambda *refs: sweep_body(first, last, len(ins), len(extra), *refs),
            out_shape=kept + outs,
            in_specs=[vmem()] * (PARTS + len(ins) + len(extra)),
            out_specs=(vmem(),) * (len(kept) + len(outs)),
            input_output_aliases={k: k for k in range(len(kept))},
            compiler_params=grant(16),
            name="sweep_first" if first else "sweep_last" if last else "sweep",
        )(*kernel, *ins, *extra)
        return (result[:PARTS] if kept else kernel), result[-1]

    ins = everyone(local_peak)
    far = swap(near, "dp", bits[-1])
    near_other = swap(near, "proto", 1)
    far_other = swap(far, "proto", 1)
    stats = None
    for it in range(ITERS):
        extra = (near, far) if it == ITERS - 2 else ()
        kernel, row_part = sweep(kernel, ins, extra, it)
        ins = everyone(row_part)
        if extra:
            stats = ins

    def final(body, operands, shape, scratch, mib, name):
        return pl.pallas_call(
            lambda *refs: body(len(ins), *refs),
            out_shape=jax.ShapeDtypeStruct(shape, f32),
            in_specs=[vmem()] * (PARTS + 2 * len(ins) + len(operands)) + [smem()],
            out_specs=vmem(),
            scratch_shapes=scratch,
            compiler_params=grant(16),
            name=name,
        )(*kernel, *ins, *stats, *operands, place)

    pair = [pltpu.VMEM((1024, LANES), f32), pltpu.VMEM((1024, LANES), bf16)]
    own_part = final(
        own_grad_body,
        (near, near_other, weight_t),
        (own, depth),
        [pltpu.VMEM((own, depth), bf16)] + pair * 2,
        4,
        "own_grad",
    )
    parts = everyone(own_part)
    pair = [pltpu.VMEM((512, rows), f32), pltpu.VMEM((512, rows), bf16)]
    proto_grad = final(
        proto_grad_body,
        (near, near_other, far, far_other, weight_t),
        (depth // n_dp, cols),
        [pltpu.VMEM((rows, depth), bf16)] + pair * 2,
        10,
        "proto_grad",
    )
    feature_grad = fold(parts, jnp.add)
    return (proto_grad, feature_grad)


def solution(mesh):
    n_dp = mesh.shape["dp"]
    n_proto = mesh.shape["proto"]

    def shards(teacher_feat, student_feat, proto_weight):
        own, depth = teacher_feat.shape
        cols = proto_weight.shape[1]
        fits = (
            own * n_dp * cols * 4 <= KERNEL_BYTES
            and own == LANES
            and depth == LANES
            and cols % (PARTS * 1024) == 0
            and n_dp & (n_dp - 1) == 0
            and n_proto & (n_proto - 1) == 0
            and 2 <= n_proto <= 8
            and depth % (n_dp * SUB) == 0
        )
        plan = all_crops if fits else split_crops
        return plan(teacher_feat, student_feat, proto_weight)

    return jax.shard_map(
        shards,
        mesh=mesh,
        in_specs=(P("dp", None), P("dp", None), P(None, "proto")),
        out_specs=(P("dp", "proto"), P("dp", None)),
        check_vma=False,
    )
```

```python
import math

import jax
import jax.numpy as jnp
from jax import lax
from jax.experimental import pallas as pl
from jax.experimental.pallas import tpu as pltpu
from jax.sharding import PartitionSpec as P

ITERS = 3

teacher_temp = 0.07
student_temp = 0.1

LOG2E = math.log2(math.e)
T_EXP = LOG2E / teacher_temp
S_EXP = LOG2E / student_temp

LANES = 128
SUB = 8
PARTS = 4
STAT_ROWS = 8
KERNEL_BYTES = 32 << 20


def combined_all(value, axis, combine):
    everything = jax.tree.map(lambda part: lax.all_gather(part, axis), value)
    leading = jax.tree.map(lambda part: part[0], everything)

    def step(k, so_far):
        return combine(so_far, jax.tree.map(lambda part: part[k], everything))

    return lax.fori_loop(1, lax.axis_size(axis), step, leading)


def divided_logits(features, prototypes, divisor):
    return jnp.dot(features, prototypes, preferred_element_type=jnp.float32) / divisor


def combine_stats(earlier, later):
    teacher_peak = jnp.maximum(earlier[0], later[0])
    student_peak = jnp.maximum(earlier[1], later[1])
    merged_total = earlier[2] * jnp.exp(earlier[1] - student_peak) + later[2] * jnp.exp(
        later[1] - student_peak
    )
    return (teacher_peak, student_peak, merged_total)


def split_crops(teacher_feat, student_feat, proto_weight):
    teacher_scores = divided_logits(teacher_feat, proto_weight, teacher_temp)
    student_scores = divided_logits(student_feat, proto_weight, student_temp)
    local_teacher = jnp.max(teacher_scores, axis=1)
    local_student = jnp.max(student_scores, axis=1)
    local_total = jnp.sum(jnp.exp(student_scores - local_student[:, None]), axis=1)
    teacher_peak, student_peak, student_total = combined_all(
        (local_teacher, local_student, local_total), "proto", combine_stats
    )
    kernel = jnp.exp(teacher_scores - teacher_peak[:, None])
    row_scale = jnp.ones((teacher_feat.shape[0],), jnp.float32)
    for sweep in range(ITERS):
        col_part = jnp.sum(kernel * row_scale[:, None], axis=0)
        col_scale = 1.0 / lax.psum(col_part, "dp")
        row_part = jnp.sum(kernel * col_scale[None, :], axis=1)
        row_scale = 1.0 / lax.psum(row_part, "proto")
    target = kernel * row_scale[:, None] * col_scale[None, :]
    student_probs = jnp.exp(student_scores - student_peak[:, None]) / student_total[:, None]
    grad_scores = ((student_probs - target) / student_temp).astype(jnp.bfloat16)
    input_part = lax.dot_general(
        grad_scores, proto_weight, (((1,), (1,)), ((), ())), preferred_element_type=jnp.float32
    )
    feature_grad = lax.psum(input_part, "proto")
    proto_grad = lax.psum_scatter(
        lax.dot_general(
            student_feat, grad_scores, (((0,), (0,)), ((), ())), preferred_element_type=jnp.float32
        ),
        "dp",
        scatter_dimension=0,
        tiled=True,
    )
    return (proto_grad, feature_grad)


def vmem():
    return pl.BlockSpec(memory_space=pltpu.VMEM)


def smem():
    return pl.BlockSpec(memory_space=pltpu.SMEM)


def swap(x, axis, bit):
    return lax.ppermute(x, axis, [(i, i ^ bit) for i in range(lax.axis_size(axis))])


def fold(parts, op):
    parts = list(parts)
    while len(parts) > 1:
        parts = [op(*parts[k : k + 2]) if k + 1 < len(parts) else parts[k] for k in range(0, len(parts), 2)]
    return parts[0]


NT = (((1,), (1,)), ((), ()))
TN = (((0,), (0,)), ((), ()))


def fold_rows(x, op):
    return fold([x[k : k + SUB, :] for k in range(0, x.shape[0], SUB)], op)


def lane_rows(flat):
    return [jnp.broadcast_to(flat[q : q + 1, :], (SUB, LANES)) for q in range(flat.shape[0])]


def own_body(place_ref, s_ref, w_ref, out_ref, wt_ref, scores_ref):
    rows = s_ref.shape[0]
    half = rows // 2
    count, width, unused = scores_ref.shape
    s = s_ref[...]
    top = None
    for j in range(count):
        wt = w_ref[:, j * width : (j + 1) * width].astype(jnp.float32).T.astype(jnp.bfloat16)
        wt_ref[j * width : (j + 1) * width, :] = wt
        scores = lax.dot_general(wt, s, NT, preferred_element_type=jnp.float32)
        scores_ref[j] = scores
        new = fold_rows(scores, jnp.maximum)
        top = new if top is None else jnp.maximum(top, new)
    peak = jnp.max(top, axis=0, keepdims=True)

    def total(j, so_far):
        return so_far + fold_rows(jnp.exp2((scores_ref[j] - peak) * S_EXP), jnp.add)

    sums = lax.fori_loop(0, count, total, jnp.zeros((SUB, rows), jnp.float32))
    first = pl.multiple_of(place_ref[0] * half, half)
    out_ref[0:half, :] = s_ref[pl.ds(first, half), :].astype(jnp.float32)
    stats = [
        peak,
        jnp.sum(sums, axis=0, keepdims=True),
        jnp.zeros((STAT_ROWS - 2, LANES), jnp.float32),
    ]
    out_ref[half:, :] = jnp.concatenate(stats, axis=0)


def join_halves(core, mine, other, out_ref, first):
    half = LANES // 2
    for j in range(mine.shape[0]):
        base = (first + j) * LANES
        a = pl.multiple_of(base + core * half, half)
        b = pl.multiple_of(base + (1 - core) * half, half)
        out_ref[pl.ds(a, half), :] = mine[j, 0:half, :].astype(jnp.bfloat16)
        out_ref[pl.ds(b, half), :] = other[j, 0:half, :].astype(jnp.bfloat16)


def scores_body(place_ref, mine_ref, other_ref, wt_ref, *refs):
    k_refs = refs[:PARTS]
    max_ref, t_scr, acc_ref = refs[PARTS:]
    join_halves(place_ref[0], mine_ref, other_ref, t_scr, 0)
    t = t_scr[...]
    per = k_refs[0].shape[0]
    chunk = min(per, 1024)
    acc_ref[...] = jnp.full(acc_ref.shape, -jnp.inf, jnp.float32)
    for p in range(PARTS):

        def block(j, unused, p=p):
            at = pl.ds(pl.multiple_of(j * chunk, chunk), chunk)
            w = wt_ref[pl.ds(pl.multiple_of(p * per + j * chunk, chunk), chunk), :]
            s = lax.dot_general(w, t, NT, preferred_element_type=jnp.float32) * T_EXP
            k_refs[p][at, :] = s
            acc_ref[...] = jnp.maximum(acc_ref[...], fold_rows(s, jnp.maximum))
            return 0

        lax.fori_loop(0, per // chunk, block, 0)
    n = max_ref.shape[0]
    tops = [jnp.max(acc_ref[:, q * LANES : (q + 1) * LANES], axis=0, keepdims=True) for q in range(n)]
    max_ref[...] = jnp.concatenate(tops, axis=0)


def sweep_body(first, last, n_in, n_extra, *refs):
    k_refs, refs = refs[:PARTS], refs[PARTS:]
    in_refs, refs = refs[:n_in], refs[n_in:]
    extra_refs, refs = refs[:n_extra], refs[n_extra:]
    if first or last:
        k_refs, refs = refs[:PARTS], refs[PARTS:]
    o_ref, y_scr = refs
    per, rows = k_refs[0].shape
    n = rows // LANES
    if first:
        scale = fold([x[...] for x in in_refs], jnp.maximum)
    else:
        scale = 1.0 / fold([x[0:n, :] for x in in_refs], jnp.add)
    wide = lane_rows(scale)
    unroll = 32
    chunk = unroll * SUB
    tiles = [slice(q * LANES, (q + 1) * LANES) for q in range(n)]

    def rows_of(i, u):
        return pl.ds(pl.multiple_of(i * chunk, chunk) + u * SUB, SUB)

    def stepped(group, load, use, carry):
        ahead = [load(u) for u in range(group)]
        for g in range(0, unroll, group):
            now = ahead
            if g + group < unroll:
                ahead = [load(u) for u in range(g + group, g + 2 * group)]
            for k, x in enumerate(now):
                carry = use(g + k, x, carry)
        return carry

    for p in range(PARTS):

        def down(i, unused, p=p):
            def load(u):
                x = [k_refs[p][rows_of(i, u), lanes] for lanes in tiles]
                return [x[q] - wide[q] if first else x[q] * wide[q] for q in range(n)]

            def use(u, x, carry):
                if first:
                    x = [jnp.exp2(v) for v in x]
                    for q in range(n):
                        k_refs[p][rows_of(i, u), tiles[q]] = x[q]
                at = pl.ds(pl.multiple_of(p * per + i * chunk, chunk) + u * SUB, SUB)
                y_scr[at, :] = fold(x, jnp.add)
                return carry

            stepped(4 if first else 1, load, use, None)
            return 0

        lax.fori_loop(0, per // chunk, down, 0)

    ones = jnp.ones((LANES, LANES), jnp.bfloat16)

    def invert(i, unused):
        at = pl.ds(pl.multiple_of(i * 1024, 1024), 1024)
        y = y_scr[at, :]
        high = y.astype(jnp.bfloat16)
        low = (y - high.astype(jnp.float32)).astype(jnp.bfloat16)
        total = jnp.dot(high, ones, preferred_element_type=jnp.float32)
        total = total + jnp.dot(low, ones, preferred_element_type=jnp.float32)
        y_scr[at, :] = 1.0 / total
        return 0

    lax.fori_loop(0, PARTS * per // 1024, invert, 0)
    acc = (jnp.zeros((SUB, LANES), jnp.float32),) * n
    for p in range(PARTS):

        def across(i, acc, p=p):
            def load(u):
                at = pl.ds(pl.multiple_of(p * per + i * chunk, chunk) + u * SUB, SUB)
                inverse = y_scr[at, :]
                return [k_refs[p][rows_of(i, u), lanes] * inverse for lanes in tiles]

            def use(u, x, acc):
                if last:
                    for q in range(n):
                        k_refs[p][rows_of(i, u), tiles[q]] = x[q]
                return tuple(acc[q] + x[q] for q in range(n))

            return stepped(2 if last else 1, load, use, acc)

        acc = lax.fori_loop(0, per // chunk, across, acc)
    o_ref[0:n, :] = jnp.concatenate([jnp.sum(x, axis=0, keepdims=True) for x in acc], axis=0)
    if n_extra:
        half = LANES // 2
        for k in range(2):
            rows_k = [x[j, half + k : half + k + 1, :] for x in extra_refs for j in range(x.shape[0])]
            o_ref[(k + 1) * n : (k + 2) * n, :] = jnp.concatenate(rows_k, axis=0)


def final_scales(row_refs, stat_refs):
    n = row_refs[0].shape[0]
    row_scale = 1.0 / fold([x[...] for x in row_refs], jnp.add)
    peak = fold([x[n : 2 * n, :] for x in stat_refs], jnp.maximum)
    total = fold(
        [x[2 * n :, :] * jnp.exp2((x[n : 2 * n, :] - peak) * S_EXP) for x in stat_refs], jnp.add
    )
    shift = peak * S_EXP + jnp.log(total * student_temp) * LOG2E
    return row_scale * (1.0 / student_temp), shift


def grad_rows(k_ref, first, s_scr, g_scr, scale, shift):
    step = 2 * SUB
    scale = [jnp.concatenate([x, x], axis=0) for x in scale]
    shift = [jnp.concatenate([x, x], axis=0) for x in shift]
    for i in range(0, s_scr.shape[0], step):
        for q in range(len(scale)):
            lanes = slice(q * LANES, (q + 1) * LANES)
            probs = jnp.exp2(s_scr[i : i + step, lanes] * S_EXP - shift[q])
            target = k_ref[pl.ds(first + i, step), lanes] * scale[q]
            g_scr[i : i + step, lanes] = (probs - target).astype(jnp.bfloat16)


def own_grad_body(n_in, *refs):
    k_refs, refs = refs[:PARTS], refs[PARTS:]
    row_refs, refs = refs[:n_in], refs[n_in:]
    stat_refs, refs = refs[:n_in], refs[n_in:]
    near_ref, other_ref, wt_ref, place_ref, out_ref, f_scr, *pairs = refs
    scale, shift = final_scales(row_refs, stat_refs)
    scale, shift = lane_rows(scale[0:1]), lane_rows(shift[0:1])
    join_halves(place_ref[0], near_ref.at[0:1], other_ref.at[0:1], f_scr, 0)
    s = f_scr[...]
    per = k_refs[0].shape[0]
    half = len(pairs) // 2
    chunk = pairs[0].shape[0]
    total = jnp.zeros(out_ref.shape, jnp.float32)
    for p in range(PARTS):
        for k in range(per // chunk):
            s_scr, g_scr = pairs[2 * (k % half)], pairs[2 * (k % half) + 1]
            start = p * per + k * chunk
            w = wt_ref[start : start + chunk, :]
            s_scr[...] = lax.dot_general(w, s, NT, preferred_element_type=jnp.float32)
            grad_rows(k_refs[p], k * chunk, s_scr, g_scr, scale, shift)
            total = total + lax.dot_general(g_scr[...], w, TN, preferred_element_type=jnp.float32)
    out_ref[...] = total


def proto_grad_body(n_in, *refs):
    k_refs, refs = refs[:PARTS], refs[PARTS:]
    row_refs, refs = refs[:n_in], refs[n_in:]
    stat_refs, refs = refs[:n_in], refs[n_in:]
    near_ref, near_other_ref, far_ref, far_other_ref, wt_ref, place_ref, out_ref = refs[:7]
    f_scr, s_even, g_even, s_odd, g_odd = refs[7:]
    scale, shift = (lane_rows(x) for x in final_scales(row_refs, stat_refs))
    core = place_ref[0]
    join_halves(core, near_ref, near_other_ref, f_scr, 0)
    join_halves(core, far_ref, far_other_ref, f_scr, near_ref.shape[0])
    s = f_scr[...]
    owned = out_ref.shape[0]
    depth = s.shape[1]
    column = lax.broadcasted_iota(jnp.int32, (depth, LANES), 1)
    wanted = column + place_ref[1] * owned
    pick = (lax.broadcasted_iota(jnp.int32, (depth, LANES), 0) == wanted) & (column < owned)
    pick = pick.astype(jnp.float32).astype(jnp.bfloat16)
    picked = jnp.dot(s, pick, preferred_element_type=jnp.float32).astype(jnp.bfloat16)
    per = k_refs[0].shape[0]
    chunk = s_even.shape[0]
    final_chunk = wt_ref.shape[0] // chunk - 1

    def scores(k, s_scr):
        at = pl.ds(pl.multiple_of(jnp.minimum(k, final_chunk) * chunk, chunk), chunk)
        s_scr[...] = lax.dot_general(wt_ref[at, :], s, NT, preferred_element_type=jnp.float32)

    def finish(k, g_scr):
        at = pl.ds(pl.multiple_of(jnp.maximum(k, 0) * chunk, chunk), chunk)
        part = jnp.dot(g_scr[...], picked, preferred_element_type=jnp.float32)
        out_ref[:, at] = part.T[0:owned, :]

    g_odd[...] = jnp.zeros_like(g_odd)
    scores(0, s_even)
    pairs = per // chunk // 2
    for p in range(PARTS):

        def step(i, unused, p=p):
            k = 2 * (p * pairs + i)
            here = pl.multiple_of(2 * i * chunk, 2 * chunk)
            scores(k + 1, s_odd)
            finish(k - 1, g_odd)
            grad_rows(k_refs[p], here, s_even, g_even, scale, shift)
            scores(k + 2, s_even)
            finish(k, g_even)
            grad_rows(k_refs[p], here + chunk, s_odd, g_odd, scale, shift)
            return 0

        lax.fori_loop(0, pairs, step, 0)
    finish(final_chunk, g_odd)


def all_crops(teacher_feat, student_feat, proto_weight):
    own, depth = teacher_feat.shape
    n_dp = lax.axis_size("dp")
    n_proto = lax.axis_size("proto")
    rows = own * n_dp
    n = rows // LANES
    cols = proto_weight.shape[1]
    per = cols // PARTS
    half = own // 2
    f32 = jnp.float32
    bf16 = jnp.bfloat16

    def grant(mib):
        return pltpu.CompilerParams(vmem_limit_bytes=mib << 20)

    place = jnp.stack([lax.axis_index("proto") % 2, lax.axis_index("dp")]).astype(jnp.int32)

    def everyone(x):
        return [x] + [swap(x, "proto", k) for k in range(1, n_proto)]

    def spread(x, bits):
        for bit in bits:
            x = jnp.concatenate([x, swap(x, "dp", bit)], axis=0)
        return x

    bits = [1 << k for k in range(n_dp.bit_length() - 1)][::-1]
    teacher_half = lax.dynamic_slice_in_dim(teacher_feat, place[0] * half, half, 0).astype(f32)
    mine = spread(teacher_half[None], bits)
    other = swap(mine, "proto", 1)

    chunk = 1024
    student_part, weight_t = pl.pallas_call(
        own_body,
        out_shape=(
            jax.ShapeDtypeStruct((half + STAT_ROWS, depth), f32),
            pltpu.VMEM((cols, depth), bf16),
        ),
        in_specs=[smem(), vmem(), vmem()],
        out_specs=(vmem(),) * 2,
        scratch_shapes=[pltpu.VMEM((cols // chunk, chunk, own), f32)],
        compiler_params=grant(16),
        name="own_stats",
    )(place, student_feat, proto_weight)
    near = spread(student_part[None], bits[:-1])

    k_shape = pltpu.VMEM((per, rows), f32)
    flat = jax.ShapeDtypeStruct((n, LANES), f32)
    *kernel, local_peak = pl.pallas_call(
        scores_body,
        out_shape=(k_shape,) * PARTS + (flat,),
        in_specs=[smem(), vmem(), vmem(), vmem()],
        out_specs=(vmem(),) * (PARTS + 1),
        scratch_shapes=[pltpu.VMEM((rows, depth), bf16), pltpu.VMEM((SUB, rows), f32)],
        compiler_params=grant(16),
        name="scores",
    )(place, mine, other, weight_t)

    def sweep(kernel, ins, extra, it):
        first, last = it == 0, it == ITERS - 1
        kept = (k_shape,) * PARTS if first or last else ()
        outs = (jax.ShapeDtypeStruct((3 * n if extra else n, LANES), f32),)
        result = pl.pallas_call(
            lambda *refs: sweep_body(first, last, len(ins), len(extra), *refs),
            out_shape=kept + outs,
            in_specs=[vmem()] * (PARTS + len(ins) + len(extra)),
            out_specs=(vmem(),) * (len(kept) + len(outs)),
            scratch_shapes=[pltpu.VMEM((cols, LANES), f32)],
            input_output_aliases={k: k for k in range(len(kept))},
            compiler_params=grant(16),
            name="sweep_first" if first else "sweep_last" if last else "sweep",
        )(*kernel, *ins, *extra)
        return (result[:PARTS] if kept else kernel), result[-1]

    ins = everyone(local_peak)
    far = swap(near, "dp", bits[-1])
    near_other = swap(near, "proto", 1)
    far_other = swap(far, "proto", 1)
    stats = None
    for it in range(ITERS):
        extra = (near, far) if it == ITERS - 2 else ()
        kernel, row_part = sweep(kernel, ins, extra, it)
        ins = everyone(row_part)
        if extra:
            stats = ins

    def final(body, operands, shape, scratch, mib, name):
        return pl.pallas_call(
            lambda *refs: body(len(ins), *refs),
            out_shape=jax.ShapeDtypeStruct(shape, f32),
            in_specs=[vmem()] * (PARTS + 2 * len(ins) + len(operands)) + [smem()],
            out_specs=vmem(),
            scratch_shapes=scratch,
            compiler_params=grant(16),
            name=name,
        )(*kernel, *ins, *stats, *operands, place)

    pair = [pltpu.VMEM((1024, LANES), f32), pltpu.VMEM((1024, LANES), bf16)]
    own_part = final(
        own_grad_body,
        (near, near_other, weight_t),
        (own, depth),
        [pltpu.VMEM((own, depth), bf16)] + pair * 2,
        4,
        "own_grad",
    )
    parts = everyone(own_part)
    pair = [pltpu.VMEM((512, rows), f32), pltpu.VMEM((512, rows), bf16)]
    proto_grad = final(
        proto_grad_body,
        (near, near_other, far, far_other, weight_t),
        (depth // n_dp, cols),
        [pltpu.VMEM((rows, depth), bf16)] + pair * 2,
        10,
        "proto_grad",
    )
    feature_grad = fold(parts, jnp.add)
    return (proto_grad, feature_grad)


def solution(mesh):
    n_dp = mesh.shape["dp"]
    n_proto = mesh.shape["proto"]

    def shards(teacher_feat, student_feat, proto_weight):
        own, depth = teacher_feat.shape
        cols = proto_weight.shape[1]
        fits = (
            own * n_dp * cols * 4 <= KERNEL_BYTES
            and own == LANES
            and depth == LANES
            and cols % (PARTS * 1024) == 0
            and n_dp & (n_dp - 1) == 0
            and n_proto & (n_proto - 1) == 0
            and 2 <= n_proto <= 8
            and depth % (n_dp * SUB) == 0
        )
        plan = all_crops if fits else split_crops
        return plan(teacher_feat, student_feat, proto_weight)

    return jax.shard_map(
        shards,
        mesh=mesh,
        in_specs=(P("dp", None), P("dp", None), P(None, "proto")),
        out_specs=(P("dp", "proto"), P("dp", None)),
        check_vma=False,
    )
```

```python
import math

import jax
import jax.numpy as jnp
from jax import lax
from jax.experimental import pallas as pl
from jax.experimental.pallas import tpu as pltpu
from jax.sharding import PartitionSpec as P


ITERS = 3

teacher_temp = 0.07
student_temp = 0.1

LOG2E = math.log2(math.e)
T_EXP = LOG2E / teacher_temp
S_EXP = LOG2E / student_temp

LANES = 128
SUB = 8
PARTS = 4
STAT_ROWS = 8
KERNEL_BYTES = 32 << 20


def combined_all(value, axis, combine):
    everything = jax.tree.map(lambda part: lax.all_gather(part, axis), value)
    leading = jax.tree.map(lambda part: part[0], everything)

    def step(k, so_far):
        return combine(so_far, jax.tree.map(lambda part: part[k], everything))

    return lax.fori_loop(1, lax.axis_size(axis), step, leading)


def divided_logits(features, prototypes, divisor):
    return jnp.dot(features, prototypes, preferred_element_type=jnp.float32) / divisor


def combine_stats(earlier, later):
    teacher_peak = jnp.maximum(earlier[0], later[0])
    student_peak = jnp.maximum(earlier[1], later[1])
    merged_total = earlier[2] * jnp.exp(earlier[1] - student_peak) + later[2] * jnp.exp(
        later[1] - student_peak
    )
    return (teacher_peak, student_peak, merged_total)


def split_crops(teacher_feat, student_feat, proto_weight):
    teacher_scores = divided_logits(teacher_feat, proto_weight, teacher_temp)
    student_scores = divided_logits(student_feat, proto_weight, student_temp)
    local_teacher = jnp.max(teacher_scores, axis=1)
    local_student = jnp.max(student_scores, axis=1)
    local_total = jnp.sum(jnp.exp(student_scores - local_student[:, None]), axis=1)
    teacher_peak, student_peak, student_total = combined_all(
        (local_teacher, local_student, local_total), "proto", combine_stats
    )
    kernel = jnp.exp(teacher_scores - teacher_peak[:, None])
    row_scale = jnp.ones((teacher_feat.shape[0],), jnp.float32)
    for _ in range(ITERS):
        col_part = jnp.sum(kernel * row_scale[:, None], axis=0)
        col_scale = 1.0 / lax.psum(col_part, "dp")
        row_part = jnp.sum(kernel * col_scale[None, :], axis=1)
        row_scale = 1.0 / lax.psum(row_part, "proto")
    target = kernel * row_scale[:, None] * col_scale[None, :]
    student_probs = jnp.exp(student_scores - student_peak[:, None]) / student_total[:, None]
    grad_scores = ((student_probs - target) / student_temp).astype(jnp.bfloat16)
    input_part = lax.dot_general(
        grad_scores, proto_weight, (((1,), (1,)), ((), ())), preferred_element_type=jnp.float32
    )
    feature_grad = lax.psum(input_part, "proto")
    proto_grad = lax.psum_scatter(
        lax.dot_general(
            student_feat, grad_scores, (((0,), (0,)), ((), ())), preferred_element_type=jnp.float32
        ),
        "dp",
        scatter_dimension=0,
        tiled=True,
    )
    return (proto_grad, feature_grad)


def vmem():
    return pl.BlockSpec(memory_space=pltpu.VMEM)


def smem():
    return pl.BlockSpec(memory_space=pltpu.SMEM)


def swap(x, axis, bit):
    return lax.ppermute(x, axis, [(i, i ^ bit) for i in range(lax.axis_size(axis))])


def fold(parts, op):
    parts = list(parts)
    while len(parts) > 1:
        parts = [op(*parts[k : k + 2]) if k + 1 < len(parts) else parts[k] for k in range(0, len(parts), 2)]
    return parts[0]


NT = (((1,), (1,)), ((), ()))
TN = (((0,), (0,)), ((), ()))


def fold_rows(x, op):
    return fold([x[k : k + SUB, :] for k in range(0, x.shape[0], SUB)], op)


def lane_rows(flat):
    return [jnp.broadcast_to(flat[q : q + 1, :], (SUB, LANES)) for q in range(flat.shape[0])]


def own_body(place_ref, s_ref, w_ref, out_ref, wt_ref, scores_ref):
    rows = s_ref.shape[0]
    half = rows // 2
    count, width, _ = scores_ref.shape
    s = s_ref[...]
    top = None
    for j in range(count):
        wt = w_ref[:, j * width : (j + 1) * width].astype(jnp.float32).T.astype(jnp.bfloat16)
        wt_ref[j * width : (j + 1) * width, :] = wt
        scores = lax.dot_general(wt, s, NT, preferred_element_type=jnp.float32)
        scores_ref[j] = scores
        new = fold_rows(scores, jnp.maximum)
        top = new if top is None else jnp.maximum(top, new)
    peak = jnp.max(top, axis=0, keepdims=True)

    def total(j, so_far):
        return so_far + fold_rows(jnp.exp2((scores_ref[j] - peak) * S_EXP), jnp.add)

    sums = lax.fori_loop(0, count, total, jnp.zeros((SUB, rows), jnp.float32))
    first = pl.multiple_of(place_ref[0] * half, half)
    out_ref[0:half, :] = s_ref[pl.ds(first, half), :].astype(jnp.float32)
    stats = [
        peak,
        jnp.sum(sums, axis=0, keepdims=True),
        jnp.zeros((STAT_ROWS - 2, LANES), jnp.float32),
    ]
    out_ref[half:, :] = jnp.concatenate(stats, axis=0)


def join_halves(core, mine, other, out_ref, first):
    half = LANES // 2
    for j in range(mine.shape[0]):
        base = (first + j) * LANES
        a = pl.multiple_of(base + core * half, half)
        b = pl.multiple_of(base + (1 - core) * half, half)
        out_ref[pl.ds(a, half), :] = mine[j, 0:half, :].astype(jnp.bfloat16)
        out_ref[pl.ds(b, half), :] = other[j, 0:half, :].astype(jnp.bfloat16)


def scores_body(place_ref, mine_ref, other_ref, wt_ref, *refs):
    k_refs = refs[:PARTS]
    max_ref, t_scr, acc_ref = refs[PARTS:]
    join_halves(place_ref[0], mine_ref, other_ref, t_scr, 0)
    t = t_scr[...]
    per = k_refs[0].shape[0]
    chunk = min(per, 1024)
    acc_ref[...] = jnp.full(acc_ref.shape, -jnp.inf, jnp.float32)
    for p in range(PARTS):

        def block(j, unused, p=p):
            at = pl.ds(pl.multiple_of(j * chunk, chunk), chunk)
            w = wt_ref[pl.ds(pl.multiple_of(p * per + j * chunk, chunk), chunk), :]
            s = lax.dot_general(w, t, NT, preferred_element_type=jnp.float32) * T_EXP
            k_refs[p][at, :] = s
            acc_ref[...] = jnp.maximum(acc_ref[...], fold_rows(s, jnp.maximum))
            return 0

        lax.fori_loop(0, per // chunk, block, 0)
    n = max_ref.shape[0]
    tops = [jnp.max(acc_ref[:, q * LANES : (q + 1) * LANES], axis=0, keepdims=True) for q in range(n)]
    max_ref[...] = jnp.concatenate(tops, axis=0)


def sweep_body(first, last, n_in, n_extra, *refs):
    k_refs, refs = refs[:PARTS], refs[PARTS:]
    in_refs, refs = refs[:n_in], refs[n_in:]
    extra_refs, refs = refs[:n_extra], refs[n_extra:]
    if first or last:
        k_refs, refs = refs[:PARTS], refs[PARTS:]
    o_ref, y_scr = refs
    per, rows = k_refs[0].shape
    n = rows // LANES
    if first:
        scale = fold([x[...] for x in in_refs], jnp.maximum)
    else:
        scale = 1.0 / fold([x[0:n, :] for x in in_refs], jnp.add)
    wide = lane_rows(scale)
    unroll = 32
    chunk = unroll * SUB
    tiles = [slice(q * LANES, (q + 1) * LANES) for q in range(n)]

    def rows_of(i, u):
        return pl.ds(pl.multiple_of(i * chunk, chunk) + u * SUB, SUB)

    def stepped(group, load, use, carry):
        ahead = [load(u) for u in range(group)]
        for g in range(0, unroll, group):
            now = ahead
            if g + group < unroll:
                ahead = [load(u) for u in range(g + group, g + 2 * group)]
            for k, x in enumerate(now):
                carry = use(g + k, x, carry)
        return carry

    for p in range(PARTS):

        def down(i, unused, p=p):
            def load(u):
                x = [k_refs[p][rows_of(i, u), lanes] for lanes in tiles]
                return [x[q] - wide[q] if first else x[q] * wide[q] for q in range(n)]

            def use(u, x, carry):
                if first:
                    x = [jnp.exp2(v) for v in x]
                    for q in range(n):
                        k_refs[p][rows_of(i, u), tiles[q]] = x[q]
                at = pl.ds(pl.multiple_of(p * per + i * chunk, chunk) + u * SUB, SUB)
                y_scr[at, :] = fold(x, jnp.add)
                return carry

            stepped(4 if first else 1, load, use, None)
            return 0

        lax.fori_loop(0, per // chunk, down, 0)

    ones = jnp.ones((LANES, LANES), jnp.bfloat16)

    def invert(i, unused):
        at = pl.ds(pl.multiple_of(i * 1024, 1024), 1024)
        y = y_scr[at, :]
        high = y.astype(jnp.bfloat16)
        low = (y - high.astype(jnp.float32)).astype(jnp.bfloat16)
        total = jnp.dot(high, ones, preferred_element_type=jnp.float32)
        total = total + jnp.dot(low, ones, preferred_element_type=jnp.float32)
        y_scr[at, :] = 1.0 / total
        return 0

    lax.fori_loop(0, PARTS * per // 1024, invert, 0)
    acc = (jnp.zeros((SUB, LANES), jnp.float32),) * n
    for p in range(PARTS):

        def across(i, acc, p=p):
            def load(u):
                at = pl.ds(pl.multiple_of(p * per + i * chunk, chunk) + u * SUB, SUB)
                inverse = y_scr[at, :]
                return [k_refs[p][rows_of(i, u), lanes] * inverse for lanes in tiles]

            def use(u, x, acc):
                if last:
                    for q in range(n):
                        k_refs[p][rows_of(i, u), tiles[q]] = x[q]
                return tuple(acc[q] + x[q] for q in range(n))

            return stepped(2 if last else 1, load, use, acc)

        acc = lax.fori_loop(0, per // chunk, across, acc)
    o_ref[0:n, :] = jnp.concatenate([jnp.sum(x, axis=0, keepdims=True) for x in acc], axis=0)
    if n_extra:
        half = LANES // 2
        for k in range(2):
            rows_k = [x[j, half + k : half + k + 1, :] for x in extra_refs for j in range(x.shape[0])]
            o_ref[(k + 1) * n : (k + 2) * n, :] = jnp.concatenate(rows_k, axis=0)


def final_scales(row_refs, stat_refs):
    n = row_refs[0].shape[0]
    row_scale = 1.0 / fold([x[...] for x in row_refs], jnp.add)
    peak = fold([x[n : 2 * n, :] for x in stat_refs], jnp.maximum)
    total = fold(
        [x[2 * n :, :] * jnp.exp2((x[n : 2 * n, :] - peak) * S_EXP) for x in stat_refs], jnp.add
    )
    shift = peak * S_EXP + jnp.log(total * student_temp) * LOG2E
    return row_scale * (1.0 / student_temp), shift


def grad_rows(k_ref, first, s_scr, g_scr, scale, shift):
    step = 2 * SUB
    scale = [jnp.concatenate([x, x], axis=0) for x in scale]
    shift = [jnp.concatenate([x, x], axis=0) for x in shift]
    for i in range(0, s_scr.shape[0], step):
        for q in range(len(scale)):
            lanes = slice(q * LANES, (q + 1) * LANES)
            probs = jnp.exp2(s_scr[i : i + step, lanes] * S_EXP - shift[q])
            target = k_ref[pl.ds(first + i, step), lanes] * scale[q]
            g_scr[i : i + step, lanes] = (probs - target).astype(jnp.bfloat16)


def own_grad_body(n_in, *refs):
    k_refs, refs = refs[:PARTS], refs[PARTS:]
    row_refs, refs = refs[:n_in], refs[n_in:]
    stat_refs, refs = refs[:n_in], refs[n_in:]
    near_ref, other_ref, wt_ref, place_ref, out_ref, f_scr, *pairs = refs
    scale, shift = final_scales(row_refs, stat_refs)
    scale, shift = lane_rows(scale[0:1]), lane_rows(shift[0:1])
    join_halves(place_ref[0], near_ref.at[0:1], other_ref.at[0:1], f_scr, 0)
    s = f_scr[...]
    per = k_refs[0].shape[0]
    half = len(pairs) // 2
    chunk = pairs[0].shape[0]
    total = jnp.zeros(out_ref.shape, jnp.float32)
    for p in range(PARTS):
        for k in range(per // chunk):
            s_scr, g_scr = pairs[2 * (k % half)], pairs[2 * (k % half) + 1]
            start = p * per + k * chunk
            w = wt_ref[start : start + chunk, :]
            s_scr[...] = lax.dot_general(w, s, NT, preferred_element_type=jnp.float32)
            grad_rows(k_refs[p], k * chunk, s_scr, g_scr, scale, shift)
            total = total + lax.dot_general(g_scr[...], w, TN, preferred_element_type=jnp.float32)
    out_ref[...] = total


def proto_grad_body(n_in, *refs):
    k_refs, refs = refs[:PARTS], refs[PARTS:]
    row_refs, refs = refs[:n_in], refs[n_in:]
    stat_refs, refs = refs[:n_in], refs[n_in:]
    near_ref, near_other_ref, far_ref, far_other_ref, wt_ref, place_ref, out_ref = refs[:7]
    f_scr, s_even, g_even, s_odd, g_odd = refs[7:]
    scale, shift = (lane_rows(x) for x in final_scales(row_refs, stat_refs))
    core = place_ref[0]
    join_halves(core, near_ref, near_other_ref, f_scr, 0)
    join_halves(core, far_ref, far_other_ref, f_scr, near_ref.shape[0])
    s = f_scr[...]
    owned = out_ref.shape[0]
    depth = s.shape[1]
    column = lax.broadcasted_iota(jnp.int32, (depth, LANES), 1)
    wanted = column + place_ref[1] * owned
    pick = (lax.broadcasted_iota(jnp.int32, (depth, LANES), 0) == wanted) & (column < owned)
    pick = pick.astype(jnp.float32).astype(jnp.bfloat16)
    picked = jnp.dot(s, pick, preferred_element_type=jnp.float32).astype(jnp.bfloat16)
    per = k_refs[0].shape[0]
    chunk = s_even.shape[0]
    final_chunk = wt_ref.shape[0] // chunk - 1

    def scores(k, s_scr):
        at = pl.ds(pl.multiple_of(jnp.minimum(k, final_chunk) * chunk, chunk), chunk)
        s_scr[...] = lax.dot_general(wt_ref[at, :], s, NT, preferred_element_type=jnp.float32)

    def finish(k, g_scr):
        at = pl.ds(pl.multiple_of(jnp.maximum(k, 0) * chunk, chunk), chunk)
        part = jnp.dot(g_scr[...], picked, preferred_element_type=jnp.float32)
        out_ref[:, at] = part.T[0:owned, :]

    g_odd[...] = jnp.zeros_like(g_odd)
    scores(0, s_even)
    pairs = per // chunk // 2
    for p in range(PARTS):

        def step(i, unused, p=p):
            k = 2 * (p * pairs + i)
            here = pl.multiple_of(2 * i * chunk, 2 * chunk)
            scores(k + 1, s_odd)
            finish(k - 1, g_odd)
            grad_rows(k_refs[p], here, s_even, g_even, scale, shift)
            scores(k + 2, s_even)
            finish(k, g_even)
            grad_rows(k_refs[p], here + chunk, s_odd, g_odd, scale, shift)
            return 0

        lax.fori_loop(0, pairs, step, 0)
    finish(final_chunk, g_odd)


def all_crops(teacher_feat, student_feat, proto_weight):
    own, depth = teacher_feat.shape
    n_dp = lax.axis_size("dp")
    n_proto = lax.axis_size("proto")
    rows = own * n_dp
    n = rows // LANES
    cols = proto_weight.shape[1]
    per = cols // PARTS
    half = own // 2
    f32 = jnp.float32
    bf16 = jnp.bfloat16

    def grant(mib):
        return pltpu.CompilerParams(vmem_limit_bytes=mib << 20)

    place = jnp.stack([lax.axis_index("proto") % 2, lax.axis_index("dp")]).astype(jnp.int32)

    def everyone(x):
        return [x] + [swap(x, "proto", k) for k in range(1, n_proto)]

    def spread(x, bits):
        for bit in bits:
            y = swap(x, "dp", bit)
            x = jnp.concatenate([x, y], axis=0)
        return x

    bits = [1 << k for k in range(n_dp.bit_length() - 1)][::-1]
    teacher_half = lax.dynamic_slice_in_dim(teacher_feat, place[0] * half, half, 0).astype(f32)
    mine = spread(teacher_half[None], bits)
    other = swap(mine, "proto", 1)

    chunk = 1024
    own_stats = pl.pallas_call(
        own_body,
        out_shape=(
            jax.ShapeDtypeStruct((half + STAT_ROWS, depth), f32),
            pltpu.VMEM((cols, depth), bf16),
        ),
        in_specs=[smem(), vmem(), vmem()],
        out_specs=(vmem(),) * 2,
        scratch_shapes=[pltpu.VMEM((cols // chunk, chunk, own), f32)],
        compiler_params=grant(16),
        name="own_stats",
    )
    student_part, weight_t = own_stats(place, student_feat, proto_weight)
    near = spread(student_part[None], bits[:-1])

    k_shape = pltpu.VMEM((per, rows), f32)
    flat = jax.ShapeDtypeStruct((n, LANES), f32)
    *kernel, local_peak = pl.pallas_call(
        scores_body,
        out_shape=(k_shape,) * PARTS + (flat,),
        in_specs=[smem(), vmem(), vmem(), vmem()],
        out_specs=(vmem(),) * (PARTS + 1),
        scratch_shapes=[pltpu.VMEM((rows, depth), bf16), pltpu.VMEM((SUB, rows), f32)],
        compiler_params=grant(16),
        name="scores",
    )(place, mine, other, weight_t)

    def sweep(kernel, ins, extra, it):
        first, last = it == 0, it == ITERS - 1
        kept = (k_shape,) * PARTS if first or last else ()
        outs = (jax.ShapeDtypeStruct((3 * n if extra else n, LANES), f32),)
        result = pl.pallas_call(
            lambda *refs: sweep_body(first, last, len(ins), len(extra), *refs),
            out_shape=kept + outs,
            in_specs=[vmem()] * (PARTS + len(ins) + len(extra)),
            out_specs=(vmem(),) * (len(kept) + len(outs)),
            scratch_shapes=[pltpu.VMEM((cols, LANES), f32)],
            input_output_aliases={k: k for k in range(len(kept))},
            compiler_params=grant(16),
            name="sweep_first" if first else "sweep_last" if last else "sweep",
        )(*kernel, *ins, *extra)
        return (result[:PARTS] if kept else kernel), result[-1]

    local_peak, near = lax.optimization_barrier((local_peak, near))
    ins = everyone(local_peak)
    far = swap(near, "dp", bits[-1])
    near_other = swap(near, "proto", 1)
    stats = None
    for it in range(ITERS):
        extra = (near, far) if it == ITERS - 2 else ()
        kernel, row_part = sweep(kernel, ins, extra, it)
        if it == 0:
            row_part, far = lax.optimization_barrier((row_part, far))
            far_other = swap(far, "proto", 1)
        elif it == 1:
            row_part, far_other = lax.optimization_barrier((row_part, far_other))
        ins = everyone(row_part)
        if extra:
            stats = ins

    def final(body, operands, shape, scratch):
        return pl.pallas_call(
            lambda *refs: body(len(ins), *refs),
            out_shape=jax.ShapeDtypeStruct(shape, f32),
            in_specs=[vmem()] * (PARTS + 2 * len(ins) + len(operands)) + [smem()],
            out_specs=vmem(),
            scratch_shapes=scratch,
            compiler_params=grant(16),
        )(*kernel, *ins, *stats, *operands, place)

    pair = [pltpu.VMEM((1024, LANES), f32), pltpu.VMEM((1024, LANES), bf16)]
    own_part = final(
        own_grad_body,
        (near, near_other, weight_t),
        (own, depth),
        [pltpu.VMEM((own, depth), bf16)] + pair * 2,
    )
    parts = everyone(own_part)
    pair = [pltpu.VMEM((512, rows), f32), pltpu.VMEM((512, rows), bf16)]
    proto_grad = final(
        proto_grad_body,
        (near, near_other, far, far_other, weight_t),
        (depth // n_dp, cols),
        [pltpu.VMEM((rows, depth), bf16)] + pair * 2,
    )
    feature_grad = fold(parts, jnp.add)
    return (proto_grad, feature_grad)


def solution(mesh):
    n_dp = mesh.shape["dp"]
    n_proto = mesh.shape["proto"]

    def shards(teacher_feat, student_feat, proto_weight):
        own, depth = teacher_feat.shape
        cols = proto_weight.shape[1]
        fits = (
            own * n_dp * cols * 4 <= KERNEL_BYTES
            and own == LANES
            and depth == LANES
            and cols % (PARTS * 1024) == 0
            and n_dp & (n_dp - 1) == 0
            and n_proto & (n_proto - 1) == 0
            and 2 <= n_proto <= 8
            and depth % (n_dp * SUB) == 0
        )
        plan = all_crops if fits else split_crops
        return plan(teacher_feat, student_feat, proto_weight)

    return jax.shard_map(
        shards,
        mesh=mesh,
        in_specs=(P("dp", None), P("dp", None), P(None, "proto")),
        out_specs=(P("dp", "proto"), P("dp", None)),
        check_vma=False,
    )
```

```python
import math

import jax
import jax.numpy as jnp
from jax import lax
from jax.experimental import pallas as pl
from jax.experimental.pallas import tpu as pltpu
from jax.sharding import PartitionSpec as P


ITERS = 3

teacher_temp = 0.07
student_temp = 0.1

LOG2E = math.log2(math.e)
T_EXP = LOG2E / teacher_temp
S_EXP = LOG2E / student_temp

LANES = 128
SUB = 8
PARTS = 4
STAT_ROWS = 8
KERNEL_BYTES = 32 << 20


def combined_all(value, axis, combine):
    everything = jax.tree.map(lambda part: lax.all_gather(part, axis), value)
    leading = jax.tree.map(lambda part: part[0], everything)

    def step(k, so_far):
        return combine(so_far, jax.tree.map(lambda part: part[k], everything))

    return lax.fori_loop(1, lax.axis_size(axis), step, leading)


def divided_logits(features, prototypes, divisor):
    return jnp.dot(features, prototypes, preferred_element_type=jnp.float32) / divisor


def combine_stats(earlier, later):
    teacher_peak = jnp.maximum(earlier[0], later[0])
    student_peak = jnp.maximum(earlier[1], later[1])
    merged_total = earlier[2] * jnp.exp(earlier[1] - student_peak) + later[2] * jnp.exp(
        later[1] - student_peak
    )
    return (teacher_peak, student_peak, merged_total)


def split_crops(teacher_feat, student_feat, proto_weight):
    teacher_scores = divided_logits(teacher_feat, proto_weight, teacher_temp)
    student_scores = divided_logits(student_feat, proto_weight, student_temp)
    local_teacher = jnp.max(teacher_scores, axis=1)
    local_student = jnp.max(student_scores, axis=1)
    local_total = jnp.sum(jnp.exp(student_scores - local_student[:, None]), axis=1)
    teacher_peak, student_peak, student_total = combined_all(
        (local_teacher, local_student, local_total), "proto", combine_stats
    )
    kernel = jnp.exp(teacher_scores - teacher_peak[:, None])
    row_scale = jnp.ones((teacher_feat.shape[0],), jnp.float32)
    for _ in range(ITERS):
        col_part = jnp.sum(kernel * row_scale[:, None], axis=0)
        col_scale = 1.0 / lax.psum(col_part, "dp")
        row_part = jnp.sum(kernel * col_scale[None, :], axis=1)
        row_scale = 1.0 / lax.psum(row_part, "proto")
    target = kernel * row_scale[:, None] * col_scale[None, :]
    student_probs = jnp.exp(student_scores - student_peak[:, None]) / student_total[:, None]
    grad_scores = ((student_probs - target) / student_temp).astype(jnp.bfloat16)
    input_part = lax.dot_general(
        grad_scores, proto_weight, (((1,), (1,)), ((), ())), preferred_element_type=jnp.float32
    )
    feature_grad = lax.psum(input_part, "proto")
    proto_grad = lax.psum_scatter(
        lax.dot_general(
            student_feat, grad_scores, (((0,), (0,)), ((), ())), preferred_element_type=jnp.float32
        ),
        "dp",
        scatter_dimension=0,
        tiled=True,
    )
    return (proto_grad, feature_grad)


def vmem():
    return pl.BlockSpec(memory_space=pltpu.VMEM)


def smem():
    return pl.BlockSpec(memory_space=pltpu.SMEM)


def swap(x, axis, bit):
    return lax.ppermute(x, axis, [(i, i ^ bit) for i in range(lax.axis_size(axis))])


def fold(parts, op):
    parts = list(parts)
    while len(parts) > 1:
        parts = [op(*parts[k : k + 2]) if k + 1 < len(parts) else parts[k] for k in range(0, len(parts), 2)]
    return parts[0]


NT = (((1,), (1,)), ((), ()))
TN = (((0,), (0,)), ((), ()))


def fold_rows(x, op):
    return fold([x[k : k + SUB, :] for k in range(0, x.shape[0], SUB)], op)


def lane_rows(flat):
    return [jnp.broadcast_to(flat[q : q + 1, :], (SUB, LANES)) for q in range(flat.shape[0])]


def own_body(place_ref, s_ref, w_ref, out_ref, wt_ref, scores_ref):
    rows = s_ref.shape[0]
    half = rows // 2
    count, width, _ = scores_ref.shape
    s = s_ref[...]
    top = None
    for j in range(count):
        wt = w_ref[:, j * width : (j + 1) * width].astype(jnp.float32).T.astype(jnp.bfloat16)
        wt_ref[j * width : (j + 1) * width, :] = wt
        scores = lax.dot_general(wt, s, NT, preferred_element_type=jnp.float32)
        scores_ref[j] = scores
        new = fold_rows(scores, jnp.maximum)
        top = new if top is None else jnp.maximum(top, new)
    peak = jnp.max(top, axis=0, keepdims=True)

    def total(j, so_far):
        return so_far + fold_rows(jnp.exp2((scores_ref[j] - peak) * S_EXP), jnp.add)

    sums = lax.fori_loop(0, count, total, jnp.zeros((SUB, rows), jnp.float32))
    first = pl.multiple_of(place_ref[0] * half, half)
    out_ref[0:half, :] = s_ref[pl.ds(first, half), :].astype(jnp.float32)
    stats = [
        peak,
        jnp.sum(sums, axis=0, keepdims=True),
        jnp.zeros((STAT_ROWS - 2, LANES), jnp.float32),
    ]
    out_ref[half:, :] = jnp.concatenate(stats, axis=0)


def join_halves(core, mine, other, out_ref, first):
    half = LANES // 2
    for j in range(mine.shape[0]):
        base = (first + j) * LANES
        a = pl.multiple_of(base + core * half, half)
        b = pl.multiple_of(base + (1 - core) * half, half)
        out_ref[pl.ds(a, half), :] = mine[j, 0:half, :].astype(jnp.bfloat16)
        out_ref[pl.ds(b, half), :] = other[j, 0:half, :].astype(jnp.bfloat16)


def scores_body(place_ref, mine_ref, other_ref, wt_ref, *refs):
    k_refs = refs[:PARTS]
    max_ref, t_scr, acc_ref = refs[PARTS:]
    join_halves(place_ref[0], mine_ref, other_ref, t_scr, 0)
    t = t_scr[...]
    per = k_refs[0].shape[0]
    chunk = min(per, 1024)
    acc_ref[...] = jnp.full(acc_ref.shape, -jnp.inf, jnp.float32)
    for p in range(PARTS):

        def block(j, unused, p=p):
            at = pl.ds(pl.multiple_of(j * chunk, chunk), chunk)
            w = wt_ref[pl.ds(pl.multiple_of(p * per + j * chunk, chunk), chunk), :]
            s = lax.dot_general(w, t, NT, preferred_element_type=jnp.float32) * T_EXP
            k_refs[p][at, :] = s
            acc_ref[...] = jnp.maximum(acc_ref[...], fold_rows(s, jnp.maximum))
            return 0

        lax.fori_loop(0, per // chunk, block, 0)
    n = max_ref.shape[0]
    tops = [jnp.max(acc_ref[:, q * LANES : (q + 1) * LANES], axis=0, keepdims=True) for q in range(n)]
    max_ref[...] = jnp.concatenate(tops, axis=0)


def sweep_body(first, last, n_in, n_extra, *refs):
    k_refs, refs = refs[:PARTS], refs[PARTS:]
    in_refs, refs = refs[:n_in], refs[n_in:]
    extra_refs, refs = refs[:n_extra], refs[n_extra:]
    if first or last:
        k_refs, refs = refs[:PARTS], refs[PARTS:]
    o_ref, y_scr = refs
    per, rows = k_refs[0].shape
    n = rows // LANES
    if first:
        scale = fold([x[...] for x in in_refs], jnp.maximum)
    else:
        scale = 1.0 / fold([x[0:n, :] for x in in_refs], jnp.add)
    wide = lane_rows(scale)
    unroll = 32
    chunk = unroll * SUB
    tiles = [slice(q * LANES, (q + 1) * LANES) for q in range(n)]

    def rows_of(i, u):
        return pl.ds(pl.multiple_of(i * chunk, chunk) + u * SUB, SUB)

    def stepped(group, load, use, carry):
        ahead = [load(u) for u in range(group)]
        for g in range(0, unroll, group):
            now = ahead
            if g + group < unroll:
                ahead = [load(u) for u in range(g + group, g + 2 * group)]
            for k, x in enumerate(now):
                carry = use(g + k, x, carry)
        return carry

    for p in range(PARTS):

        def down(i, unused, p=p):
            def load(u):
                x = [k_refs[p][rows_of(i, u), lanes] for lanes in tiles]
                return [x[q] - wide[q] if first else x[q] * wide[q] for q in range(n)]

            def use(u, x, carry):
                if first:
                    x = [jnp.exp2(v) for v in x]
                    for q in range(n):
                        k_refs[p][rows_of(i, u), tiles[q]] = x[q]
                at = pl.ds(pl.multiple_of(p * per + i * chunk, chunk) + u * SUB, SUB)
                y_scr[at, :] = fold(x, jnp.add)
                return carry

            stepped(4 if first else 1, load, use, None)
            return 0

        lax.fori_loop(0, per // chunk, down, 0)

    ones = jnp.ones((LANES, LANES), jnp.bfloat16)

    def invert(i, unused):
        at = pl.ds(pl.multiple_of(i * per, per), per)
        y = y_scr[at, :]
        high = y.astype(jnp.bfloat16)
        low = (y - high.astype(jnp.float32)).astype(jnp.bfloat16)
        total = jnp.dot(high, ones, preferred_element_type=jnp.float32)
        total = total + jnp.dot(low, ones, preferred_element_type=jnp.float32)
        y_scr[at, :] = 1.0 / total
        return 0

    lax.fori_loop(0, PARTS, invert, 0)
    acc = (jnp.zeros((SUB, LANES), jnp.float32),) * n
    for p in range(PARTS):

        def across(i, acc, p=p):
            def load(u):
                at = pl.ds(pl.multiple_of(p * per + i * chunk, chunk) + u * SUB, SUB)
                inverse = y_scr[at, :]
                return [k_refs[p][rows_of(i, u), lanes] * inverse for lanes in tiles]

            def use(u, x, acc):
                if last:
                    for q in range(n):
                        k_refs[p][rows_of(i, u), tiles[q]] = x[q]
                return tuple(acc[q] + x[q] for q in range(n))

            return stepped(2 if last else 1, load, use, acc)

        acc = lax.fori_loop(0, per // chunk, across, acc)
    o_ref[0:n, :] = jnp.concatenate([jnp.sum(x, axis=0, keepdims=True) for x in acc], axis=0)
    if n_extra:
        half = LANES // 2
        for k in range(2):
            rows_k = [x[j, half + k : half + k + 1, :] for x in extra_refs for j in range(x.shape[0])]
            o_ref[(k + 1) * n : (k + 2) * n, :] = jnp.concatenate(rows_k, axis=0)


def final_scales(row_refs, stat_refs):
    n = row_refs[0].shape[0]
    row_scale = 1.0 / fold([x[...] for x in row_refs], jnp.add)
    peak = fold([x[n : 2 * n, :] for x in stat_refs], jnp.maximum)
    total = fold(
        [x[2 * n :, :] * jnp.exp2((x[n : 2 * n, :] - peak) * S_EXP) for x in stat_refs], jnp.add
    )
    shift = peak * S_EXP + jnp.log(total * student_temp) * LOG2E
    return row_scale * (1.0 / student_temp), shift


def grad_rows(k_ref, first, s_scr, g_scr, scale, shift):
    step = 2 * SUB
    scale = [jnp.concatenate([x, x], axis=0) for x in scale]
    shift = [jnp.concatenate([x, x], axis=0) for x in shift]
    for i in range(0, s_scr.shape[0], step):
        for q in range(len(scale)):
            lanes = slice(q * LANES, (q + 1) * LANES)
            probs = jnp.exp2(s_scr[i : i + step, lanes] * S_EXP - shift[q])
            target = k_ref[pl.ds(first + i, step), lanes] * scale[q]
            g_scr[i : i + step, lanes] = (probs - target).astype(jnp.bfloat16)


def own_grad_body(n_in, *refs):
    k_refs, refs = refs[:PARTS], refs[PARTS:]
    row_refs, refs = refs[:n_in], refs[n_in:]
    stat_refs, refs = refs[:n_in], refs[n_in:]
    near_ref, other_ref, wt_ref, place_ref, out_ref, f_scr, *pairs = refs
    scale, shift = final_scales(row_refs, stat_refs)
    scale, shift = lane_rows(scale[0:1]), lane_rows(shift[0:1])
    join_halves(place_ref[0], near_ref.at[0:1], other_ref.at[0:1], f_scr, 0)
    s = f_scr[...]
    per = k_refs[0].shape[0]
    half = len(pairs) // 2
    chunk = pairs[0].shape[0]
    total = jnp.zeros(out_ref.shape, jnp.float32)
    for p in range(PARTS):
        for k in range(per // chunk):
            s_scr, g_scr = pairs[2 * (k % half)], pairs[2 * (k % half) + 1]
            start = p * per + k * chunk
            w = wt_ref[start : start + chunk, :]
            s_scr[...] = lax.dot_general(w, s, NT, preferred_element_type=jnp.float32)
            grad_rows(k_refs[p], k * chunk, s_scr, g_scr, scale, shift)
            total = total + lax.dot_general(g_scr[...], w, TN, preferred_element_type=jnp.float32)
    out_ref[...] = total


def proto_grad_body(n_in, *refs):
    k_refs, refs = refs[:PARTS], refs[PARTS:]
    row_refs, refs = refs[:n_in], refs[n_in:]
    stat_refs, refs = refs[:n_in], refs[n_in:]
    near_ref, near_other_ref, far_ref, far_other_ref, wt_ref, place_ref, out_ref = refs[:7]
    f_scr, s_even, g_even, s_odd, g_odd = refs[7:]
    scale, shift = (lane_rows(x) for x in final_scales(row_refs, stat_refs))
    core = place_ref[0]
    join_halves(core, near_ref, near_other_ref, f_scr, 0)
    join_halves(core, far_ref, far_other_ref, f_scr, near_ref.shape[0])
    s = f_scr[...]
    owned = out_ref.shape[0]
    depth = s.shape[1]
    column = lax.broadcasted_iota(jnp.int32, (depth, LANES), 1)
    wanted = column + place_ref[1] * owned
    pick = (lax.broadcasted_iota(jnp.int32, (depth, LANES), 0) == wanted) & (column < owned)
    pick = pick.astype(jnp.float32).astype(jnp.bfloat16)
    picked = jnp.dot(s, pick, preferred_element_type=jnp.float32).astype(jnp.bfloat16)
    per = k_refs[0].shape[0]
    chunk = s_even.shape[0]
    final_chunk = wt_ref.shape[0] // chunk - 1

    def scores(k, s_scr):
        at = pl.ds(pl.multiple_of(jnp.minimum(k, final_chunk) * chunk, chunk), chunk)
        s_scr[...] = lax.dot_general(wt_ref[at, :], s, NT, preferred_element_type=jnp.float32)

    def finish(k, g_scr):
        at = pl.ds(pl.multiple_of(jnp.maximum(k, 0) * chunk, chunk), chunk)
        part = jnp.dot(g_scr[...], picked, preferred_element_type=jnp.float32)
        out_ref[:, at] = part.T[0:owned, :]

    g_odd[...] = jnp.zeros_like(g_odd)
    scores(0, s_even)
    pairs = per // chunk // 2
    for p in range(PARTS):

        def step(i, unused, p=p):
            k = 2 * (p * pairs + i)
            here = pl.multiple_of(2 * i * chunk, 2 * chunk)
            scores(k + 1, s_odd)
            finish(k - 1, g_odd)
            grad_rows(k_refs[p], here, s_even, g_even, scale, shift)
            scores(k + 2, s_even)
            finish(k, g_even)
            grad_rows(k_refs[p], here + chunk, s_odd, g_odd, scale, shift)
            return 0

        lax.fori_loop(0, pairs, step, 0)
    finish(final_chunk, g_odd)


def all_crops(teacher_feat, student_feat, proto_weight):
    own, depth = teacher_feat.shape
    n_dp = lax.axis_size("dp")
    n_proto = lax.axis_size("proto")
    rows = own * n_dp
    n = rows // LANES
    cols = proto_weight.shape[1]
    per = cols // PARTS
    half = own // 2
    f32 = jnp.float32
    bf16 = jnp.bfloat16

    def grant(mib):
        return pltpu.CompilerParams(vmem_limit_bytes=mib << 20)

    place = jnp.stack([lax.axis_index("proto") % 2, lax.axis_index("dp")]).astype(jnp.int32)

    def everyone(x):
        return [x] + [swap(x, "proto", k) for k in range(1, n_proto)]

    def spread(x, bits):
        for bit in bits:
            y = swap(x, "dp", bit)
            x = jnp.concatenate([x, y], axis=0)
        return x

    bits = [1 << k for k in range(n_dp.bit_length() - 1)][::-1]
    teacher_half = lax.dynamic_slice_in_dim(teacher_feat, place[0] * half, half, 0).astype(f32)
    mine = spread(teacher_half[None], bits)
    other = swap(mine, "proto", 1)

    chunk = 1024
    own_stats = pl.pallas_call(
        own_body,
        out_shape=(
            jax.ShapeDtypeStruct((half + STAT_ROWS, depth), f32),
            pltpu.VMEM((cols, depth), bf16),
        ),
        in_specs=[smem(), vmem(), vmem()],
        out_specs=(vmem(),) * 2,
        scratch_shapes=[pltpu.VMEM((cols // chunk, chunk, own), f32)],
        compiler_params=grant(16),
        name="own_stats",
    )
    student_part, weight_t = own_stats(place, student_feat, proto_weight)
    near = spread(student_part[None], bits[:-1])

    k_shape = pltpu.VMEM((per, rows), f32)
    flat = jax.ShapeDtypeStruct((n, LANES), f32)
    *kernel, local_peak = pl.pallas_call(
        scores_body,
        out_shape=(k_shape,) * PARTS + (flat,),
        in_specs=[smem(), vmem(), vmem(), vmem()],
        out_specs=(vmem(),) * (PARTS + 1),
        scratch_shapes=[pltpu.VMEM((rows, depth), bf16), pltpu.VMEM((SUB, rows), f32)],
        compiler_params=grant(16),
        name="scores",
    )(place, mine, other, weight_t)

    def sweep(kernel, ins, extra, it):
        first, last = it == 0, it == ITERS - 1
        kept = (k_shape,) * PARTS if first or last else ()
        outs = (jax.ShapeDtypeStruct((3 * n if extra else n, LANES), f32),)
        result = pl.pallas_call(
            lambda *refs: sweep_body(first, last, len(ins), len(extra), *refs),
            out_shape=kept + outs,
            in_specs=[vmem()] * (PARTS + len(ins) + len(extra)),
            out_specs=(vmem(),) * (len(kept) + len(outs)),
            scratch_shapes=[pltpu.VMEM((cols, LANES), f32)],
            input_output_aliases={k: k for k in range(len(kept))},
            compiler_params=grant(16),
            name="sweep_first" if first else "sweep_last" if last else "sweep",
        )(*kernel, *ins, *extra)
        return (result[:PARTS] if kept else kernel), result[-1]

    local_peak, near = lax.optimization_barrier((local_peak, near))
    ins = everyone(local_peak)
    far = swap(near, "dp", bits[-1])
    near_other = swap(near, "proto", 1)
    stats = None
    for it in range(ITERS):
        extra = (near, far) if it == ITERS - 2 else ()
        kernel, row_part = sweep(kernel, ins, extra, it)
        if it == 0:
            row_part, far = lax.optimization_barrier((row_part, far))
            far_other = swap(far, "proto", 1)
        elif it == 1:
            row_part, far_other = lax.optimization_barrier((row_part, far_other))
        ins = everyone(row_part)
        if extra:
            stats = ins

    def final(body, operands, shape, scratch):
        return pl.pallas_call(
            lambda *refs: body(len(ins), *refs),
            out_shape=jax.ShapeDtypeStruct(shape, f32),
            in_specs=[vmem()] * (PARTS + 2 * len(ins) + len(operands)) + [smem()],
            out_specs=vmem(),
            scratch_shapes=scratch,
            compiler_params=grant(16),
        )(*kernel, *ins, *stats, *operands, place)

    pair = [pltpu.VMEM((1024, LANES), f32), pltpu.VMEM((1024, LANES), bf16)]
    own_part = final(
        own_grad_body,
        (near, near_other, weight_t),
        (own, depth),
        [pltpu.VMEM((own, depth), bf16)] + pair * 2,
    )
    parts = everyone(own_part)
    pair = [pltpu.VMEM((1024, rows), f32), pltpu.VMEM((1024, rows), bf16)]
    proto_grad = final(
        proto_grad_body,
        (near, near_other, far, far_other, weight_t),
        (depth // n_dp, cols),
        [pltpu.VMEM((rows, depth), bf16)] + pair * 2,
    )
    feature_grad = fold(parts, jnp.add)
    return (proto_grad, feature_grad)


def solution(mesh):
    n_dp = mesh.shape["dp"]
    n_proto = mesh.shape["proto"]

    def shards(teacher_feat, student_feat, proto_weight):
        own, depth = teacher_feat.shape
        cols = proto_weight.shape[1]
        fits = (
            own * n_dp * cols * 4 <= KERNEL_BYTES
            and own == LANES
            and depth == LANES
            and cols % (PARTS * 2048) == 0
            and n_dp & (n_dp - 1) == 0
            and n_proto & (n_proto - 1) == 0
            and 2 <= n_proto <= 8
            and depth % (n_dp * SUB) == 0
        )
        plan = all_crops if fits else split_crops
        return plan(teacher_feat, student_feat, proto_weight)

    return jax.shard_map(
        shards,
        mesh=mesh,
        in_specs=(P("dp", None), P("dp", None), P(None, "proto")),
        out_specs=(P("dp", "proto"), P("dp", None)),
        check_vma=False,
    )
```
